32 devices in a mesh: grp: 4 (over y, x), leaf: 8 (over z, core).
Axes of the slice: x: 2, y: 2, z: 4, core: 2. Of those that a mesh axis runs over, the one named last changes fastest.
Arguments:
- basis: float32 [8, 65536], P(None, ('grp', 'leaf')), may hold values from -28 to 28
- roots: float32 [5], replicated, may hold values from 0.35 to 1
- near_blocks: bfloat16 [256, 6, 256, 256], P(('grp', 'leaf')), may hold values from -0.046875 to 0.046875
- near_ids: int32 [256, 6], P(('grp', 'leaf')), may hold values from 0 to 255, as said below
- leaf_basis: bfloat16 [256, 64, 256], P(('grp', 'leaf')), may hold values from -0.375 to 0.375
- far_coupling: bfloat16 [256, 8, 64, 64], P(('grp', 'leaf')), may hold values from -0.109375 to 0.109375
- far_ids: int32 [256, 8], P(('grp', 'leaf')), may hold values from 0 to 255, as said below
- transfer: bfloat16 [256, 64, 128], P(('grp', 'leaf')), may hold values from -0.5 to 0.5
- top_coupling: bfloat16 [128, 8, 128, 128], P(('grp', 'leaf')), may hold values from -0.078125 to 0.078125
- top_ids: int32 [128, 8], P(('grp', 'leaf')), may hold values from 0 to 127, as said below
Outputs:
- next_vector: float32 [65536], P(('grp', 'leaf'))
- hessen: float32 [9], replicated
The draws below stay inside these ranges and needn't reach their ends.
Inputs may be any that keep to these rules, and one draw needn't show every extreme that they name: `near_ids`: row i starts with i itself; the others lie within 8 leaves of i. `far_ids`: every entry lies within 8 leaves of its row. `top_ids`: every entry lies within 4 parents of its row.
All inputs are finite; a program needn't handle non-finite values.
Results may differ from the reference program's by a relative error of at most 0.024.
Values may be sent and summed in bfloat16 or wider, within the bound.
A program may use at most 64 MiB of HBM per device.

```python
import jax
import jax.numpy as jnp
from jax import lax

LEAF = 256
RANK = 64
PRANK = 128
LPD = 8
NEAR = 6
FAR = 8
TOPL = 8
BASIS = 8
ROOTS = 5
LEAVES = 256
PARENTS = 128
PANELS = 65536


def local_ids(key, rows_count, count, reach):
    rows = jnp.arange(rows_count, dtype=jnp.int32)[:, None]
    offsets = jax.random.randint(key, (rows_count, count), -reach, reach + 1)
    return jnp.clip(rows + offsets, 0, rows_count - 1).astype(jnp.int32)


def draw_near_ids(key, part):
    others = local_ids(jax.random.fold_in(key, 11), LEAVES, NEAR - 1, LPD)
    itself = jnp.arange(LEAVES, dtype=jnp.int32)[:, None]
    return jnp.concatenate([itself, others], axis=1).astype(jnp.int32)


def draw_far_ids(key, part):
    return local_ids(jax.random.fold_in(key, 23), LEAVES, FAR, LPD)


def draw_top_ids(key, part):
    return local_ids(jax.random.fold_in(key, 37), PARENTS, TOPL, LPD // 2)


def draw_basis(key, part):
    position = jnp.arange(PANELS, dtype=jnp.float32) / jnp.float32(PANELS)
    rising = jnp.exp2(2.0 * position)
    leaf_scale = jnp.exp(jax.random.uniform(jax.random.fold_in(key, 51), (LEAVES, 1), jnp.float32, jnp.log(0.7), jnp.log(1.4)))
    rough = jnp.broadcast_to(leaf_scale, (LEAVES, LEAF)).reshape(PANELS)
    noise = jnp.clip(jax.random.normal(jax.random.fold_in(key, 53), (BASIS, PANELS), jnp.float32), -4.0, 4.0)
    common = jnp.clip(jax.random.normal(jax.random.fold_in(key, 59), (1, PANELS), jnp.float32), -4.0, 4.0)
    values = noise + 0.4 * common
    return (values * (rising * rough)[None, :]).astype(jnp.float32)


def shard_levels(key, extent, split, low, largest):
    level, own = 1.0, jax.random.fold_in(key, 6)
    for dim, blocks in split:
        draws = jnp.exp(jax.random.uniform(jax.random.fold_in(own, dim), (blocks,), jnp.float32, low / len(split), largest / len(split)))
        level = level * jnp.repeat(draws, extent[dim] // blocks).reshape([-1 if axis == dim else 1 for axis in range(len(extent))])
    return level


def gaussian(rng, extent, scale, bound, split=(), kind=jnp.bfloat16):
    values = scale * jax.random.normal(rng, extent, jnp.float32)
    if split:
        values = values * shard_levels(rng, extent, split, -0.22, 0.18)
    return jnp.clip(values, -bound, bound).astype(kind)


def setup_inputs(seed: int = 0) -> dict:
    seeds = jax.random.split(jax.random.key(seed), 11)
    basis = draw_basis(jax.random.fold_in(seeds[10], 71), 0)
    roots = jnp.clip(jax.random.uniform(seeds[1], (ROOTS,), jnp.float32, 0.35, 1.0), 0.35, 1.0)
    near_blocks = gaussian(seeds[2], (LEAVES, NEAR, LEAF, LEAF), (LEAF * NEAR * 11) ** -0.5, 0.046875, ((0, 32),))
    near_ids = draw_near_ids(jax.random.fold_in(seeds[10], 71), 0)
    leaf_basis = gaussian(seeds[4], (LEAVES, RANK, LEAF), LEAF ** -0.5, 0.375, ((0, 32),))
    far_coupling = gaussian(seeds[5], (LEAVES, FAR, RANK, RANK), (FAR * RANK * 6) ** -0.5, 0.109375, ((0, 32),))
    far_ids = draw_far_ids(jax.random.fold_in(seeds[10], 71), 0)
    transfer = gaussian(seeds[7], (LEAVES, RANK, PRANK), (2 * RANK) ** -0.5, 0.5, ((0, 32),))
    top_coupling = gaussian(seeds[8], (PARENTS, TOPL, PRANK, PRANK), (TOPL * PRANK * 6) ** -0.5, 0.078125, ((0, 32),))
    top_ids = draw_top_ids(jax.random.fold_in(seeds[10], 71), 0)
    return dict(basis=basis, roots=roots, near_blocks=near_blocks, near_ids=near_ids, leaf_basis=leaf_basis, far_coupling=far_coupling, far_ids=far_ids, transfer=transfer, top_coupling=top_coupling, top_ids=top_ids)


def apply_operator(field, near_blocks, near_ids, leaf_basis, far_coupling, far_ids, transfer, top_coupling, top_ids):
    rounded = field.astype(jnp.bfloat16)
    groups = LEAVES // LPD

    def near_piece(pieces):
        blocks, indices = pieces
        nearby = rounded[indices].astype(jnp.float32)
        return jnp.einsum('lkab,lkb->la', blocks.astype(jnp.float32), nearby)
    near_term = lax.map(near_piece, (near_blocks.reshape(groups, LPD, NEAR, LEAF, LEAF), near_ids.reshape(groups, LPD, NEAR)))
    near_term = near_term.reshape(LEAVES, LEAF)
    coeffs = jnp.einsum('lra,la->lr', leaf_basis.astype(jnp.float32), rounded.astype(jnp.float32)).astype(jnp.bfloat16)
    partners = coeffs[far_ids].astype(jnp.float32)
    leaf_sum = jnp.einsum('lkrs,lks->lr', far_coupling.astype(jnp.float32), partners)
    upward = jnp.einsum('lrp,lr->lp', transfer.astype(jnp.float32), coeffs.astype(jnp.float32))
    upward = upward.reshape(PARENTS, 2, PRANK).sum(1).astype(jnp.bfloat16)
    sources = upward[top_ids].astype(jnp.float32)
    top_sum = jnp.einsum('pkab,pkb->pa', top_coupling.astype(jnp.float32), sources).astype(jnp.bfloat16)
    down = jnp.einsum('lrp,lp->lr', transfer.astype(jnp.float32), jnp.repeat(top_sum, 2, axis=0).astype(jnp.float32))
    local_coef = (leaf_sum + down).astype(jnp.bfloat16)
    far_term = jnp.einsum('lra,lr->la', leaf_basis.astype(jnp.float32), local_coef.astype(jnp.float32))
    return 0.5 * field + near_term + far_term

def reference(basis, roots, near_blocks, near_ids, leaf_basis, far_coupling, far_ids, transfer, top_coupling, top_ids):

    def operator(field):
        return apply_operator(field, near_blocks, near_ids, leaf_basis, far_coupling, far_ids, transfer, top_coupling, top_ids)
    vectors = basis.reshape(BASIS, LEAVES, LEAF)
    product = vectors[BASIS - 1]
    result = jnp.zeros_like(product)
    for index in range(ROOTS):
        result = result + product / roots[index]
        if index < ROOTS - 1:
            product = product - operator(product) / roots[index]
    image = operator(result)
    total = jnp.float32(PANELS)
    hcoef = jnp.einsum('mla,la->m', vectors, image, precision=lax.Precision.HIGHEST) / total
    remain = image - jnp.einsum('m,mla->la', hcoef, vectors, precision=lax.Precision.HIGHEST)
    beta = jnp.sqrt(jnp.sum(remain * remain) / total + 1e-06)
    next_vector = (remain / beta).reshape(PANELS)
    hessen = jnp.concatenate([hcoef, beta[None]])
    return (next_vector, hessen)
```

```python
import functools

import jax
import jax.numpy as jnp
from jax import lax
from jax.experimental import pallas as pl
from jax.experimental.pallas import tpu as pltpu
from jax.sharding import PartitionSpec as P

MESH = pl.DeviceIdType.MESH
F32 = jnp.float32
BF16 = jnp.bfloat16
LANES = 128


def nt(a, b):
    return lax.dot_general(a, b, (((1,), (1,)), ((), ())), preferred_element_type=F32)


def nn(a, b):
    return lax.dot_general(a, b, (((1,), (0,)), ((), ())), preferred_element_type=F32)


def iota(shape, dim):
    return lax.broadcasted_iota(jnp.int32, shape, dim)


def kernel(
    n_grp,
    n_leaf,
    basis_hbm,
    roots_hbm,
    near_hbm,
    near_ids_hbm,
    lb_hbm,
    fc_hbm,
    far_ids_hbm,
    tr_hbm,
    tc_hbm,
    top_ids_hbm,
    out,
    hess,
    bas,
    roots,
    near,
    near_t,
    near_ids,
    lb,
    up_w,
    fc,
    fcc,
    far_ids,
    tr,
    tc,
    top_ids,
    g_w,
    near_ix,
    far_ix,
    top_ix,
    own_x,
    own_ct,
    halo_x,
    halo_ct,
    prod_buf,
    z_buf,
    w_buf,
    gram_row,
    slots,
    load_sem,
    near_sem,
    send_sem,
    recv_sem,
    red_sem,
):
    n_dev = n_grp * n_leaf
    leaves, n_near, width, _ = near.shape
    n_far, rank = fc.shape[1], fc.shape[2]
    n_top, prank = tc.shape[1], tc.shape[2]
    parents = tc.shape[0]
    count = basis_hbm.shape[0]
    steps = roots.shape[1]
    coefs = leaves * rank
    halves = width // LANES
    chunks = leaves * halves
    far_tiles = n_far * rank // LANES
    mg, ml = lax.axis_index("grp"), lax.axis_index("leaf")
    me = mg * n_leaf + ml

    def place(index):
        return (lax.div(index, n_leaf), lax.rem(index, n_leaf))

    odd = lax.rem(me, 2)
    fast = me + 1 - 2 * odd
    slow = me - 1 + 2 * odd
    has_slow = jnp.logical_and(slow >= 0, slow < n_dev)

    def others():
        for dg in range(n_grp):
            g = lax.rem(mg + dg, n_grp)
            for dl in range(n_leaf):
                if dg or dl:
                    yield (g, lax.rem(ml + dl, n_leaf))

    first = [
        pltpu.make_async_copy(
            basis_hbm.at[:, c * LANES : (c + 1) * LANES],
            bas.at[c * count : (c + 1) * count, :],
            load_sem.at[0],
        )
        for c in range(chunks)
    ]
    all_basis = pltpu.make_async_copy(bas, bas, load_sem.at[0])
    loads = [
        pltpu.make_async_copy(src, dst, load_sem.at[1 + n])
        for n, (src, dst) in enumerate(
            (
                (roots_hbm, roots),
                (near_ids_hbm, near_ids),
                (far_ids_hbm, far_ids),
                (top_ids_hbm, top_ids),
                (lb_hbm, lb),
                (tr_hbm, tr),
                (fc_hbm, fc),
                (tc_hbm, tc),
            )
        )
    ]
    lb_copy, tr_copy, fc_copy, tc_copy = loads[4:]
    for copy in first + loads:
        copy.start()
    for i in range(leaves):
        pltpu.make_async_copy(near_hbm.at[i], near.at[i], near_sem.at[i]).start()

    barrier = pltpu.get_barrier_semaphore()
    for target in others():
        pl.semaphore_signal(barrier, inc=1, device_id=target, device_id_type=MESH)

    row = iota((leaves, LANES), 0)
    lane = iota((leaves, LANES), 1)
    low = lane < rank
    even = row % 2 == 0
    own_base = me * leaves
    shift = (1 - 2 * odd) * leaves

    def side_tile(source, j, lo):
        return jnp.broadcast_to(source[j : j + 1, lo : lo + LANES], (leaves, LANES))

    @pl.when(jnp.logical_not(has_slow))
    def _():
        for step in range(steps):
            halo_x[step, 1] = jnp.zeros((leaves, width), F32)
            halo_ct[step, 1] = jnp.zeros((2 * leaves, LANES), F32)

    for copy in loads[:4]:
        copy.wait()
    nid = near_ids[...] - own_base
    for k in range(1, n_near):
        tile = jnp.broadcast_to(nid[:, k : k + 1], (leaves, LANES))
        near_ix[0, k - 1] = tile
        near_ix[1, k - 1] = tile - shift
        near_ix[2, k - 1] = tile + shift
    fid = far_ids[...] - own_base
    for v in range(far_tiles):
        tile = jnp.where(low, fid[:, 2 * v : 2 * v + 1], fid[:, 2 * v + 1 : 2 * v + 2])
        far_ix[0, v] = tile
        far_ix[1, v] = tile - shift
        far_ix[2, v] = tile + shift
    tid = jnp.zeros((leaves, n_top), jnp.int32)
    for p in range(parents):
        tid = jnp.where(iota((leaves, n_top), 0) // 2 == p, top_ids[p : p + 1, :], tid)
    tid = (tid - me * parents) * 2
    for k in range(n_top):
        tile = jnp.broadcast_to(tid[:, k : k + 1], (leaves, LANES))
        top_ix[0, k] = tile
        top_ix[1, k] = tile - shift
        top_ix[2, k] = tile + shift

    all_basis.wait()
    for h in range(halves):
        prod_buf[:, h * LANES : (h + 1) * LANES] = bas[
            pl.ds(count - 1 + count * h, leaves, stride=count * halves), :
        ]
    z_buf[...] = jnp.zeros_like(z_buf)

    lb_copy.wait()
    lb_t = lb[...].T
    up_w[:, 0:coefs] = lb_t
    tr_copy.wait()
    for i in range(leaves):
        block = nn(lb_t[:, i * rank : (i + 1) * rank], tr[i * rank : (i + 1) * rank, :])
        up_w[:, coefs + i * prank : coefs + (i + 1) * prank] = block.astype(BF16)

    pl.semaphore_wait(barrier, n_dev - 1)

    def x_copy(step, side):
        return pltpu.make_async_remote_copy(
            src_ref=own_x.at[step],
            dst_ref=halo_x.at[step, side],
            send_sem=send_sem.at[step, 0, side],
            recv_sem=recv_sem.at[step, 0, side],
            device_id=place((fast, slow)[side]),
            device_id_type=MESH,
        )

    def ct_copy(step, side):
        return pltpu.make_async_remote_copy(
            src_ref=own_ct.at[step],
            dst_ref=halo_ct.at[step, side],
            send_sem=send_sem.at[step, 1, side],
            recv_sem=recv_sem.at[step, 1, side],
            device_id=place((fast, slow)[side]),
            device_id_type=MESH,
        )

    def send(step, make):
        @pl.when(has_slow)
        def _():
            make(step, 1).start()

        make(step, 0).start()

    def receive(step, make, side):
        if side == 0:
            make(step, 0).wait_recv()
        else:

            @pl.when(has_slow)
            def _():
                make(step, 1).wait_recv()

    def pick_x(ix, source, acc):
        out = [list(a) for a in acc]
        rows = [[side_tile(source, j, h * LANES) for h in range(halves)] for j in range(leaves)]
        for k in range(n_near - 1):
            index = near_ix[ix, k]
            for j in range(leaves):
                hit = index == j
                for h in range(halves):
                    out[k][h] = jnp.where(hit, rows[j][h], out[k][h])
        return out

    def pick_ct(ix, source, far, top):
        far, top = list(far), list(top)
        for j in range(leaves):
            tile = side_tile(source, j, 0)
            for v in range(far_tiles):
                far[v] = jnp.where(far_ix[ix, v] == j, tile, far[v])
        for j in range(0, leaves, 2):
            tile = side_tile(source, leaves + j, 0)
            for k in range(n_top):
                top[k] = jnp.where(top_ix[ix, k] == j, tile, top[k])
        return far, top

    def prepare():
        def turn(i, carry):
            pltpu.make_async_copy(near_hbm.at[i], near.at[i], near_sem.at[i]).wait()
            for k in range(n_near):
                near_t[i, k] = near[i, k].T
            return carry

        lax.fori_loop(0, leaves, turn, 0)
        fc_copy.wait()
        for k in range(n_far):
            for i in range(leaves):
                fcc[i * rank : (i + 1) * rank, k * rank : (k + 1) * rank] = fc[i, k]
        g_w[0 : n_far * rank, :] = fcc[...].T
        tc_copy.wait()
        base = n_far * rank

        def fold(k, carry):
            start = pl.multiple_of(base + k * prank, prank)
            for p in range(parents):
                pair = tr[p * 2 * rank : (p + 1) * 2 * rank, :]
                block = nn(pair, tc[p, k]).astype(BF16).T
                g_w[pl.ds(start, prank), p * 2 * rank : (p + 1) * 2 * rank] = block
            return carry

        lax.fori_loop(0, n_top, fold, 0)
        flat = jnp.concatenate(
            [bas[c * count : (c + 1) * count, :] for c in range(chunks)], 1
        )
        gram = lax.dot_general(
            flat,
            flat,
            (((1,), (1,)), ((), ())),
            precision=lax.Precision.HIGHEST,
            preferred_element_type=F32,
        )
        flip = iota((count, count), 0) + iota((count, count), 1) == count - 1
        gram = lax.dot_general(
            flip.astype(F32),
            gram,
            (((1,), (0,)), ((), ())),
            precision=lax.Precision.HIGHEST,
            preferred_element_type=F32,
        )
        gram = jnp.pad(gram, ((0, 0), (0, LANES - count)))
        spread = pltpu.roll(gram, 0, 1, stride=count, stride_axis=0)
        gram_row[...] = jnp.sum(spread, 0, keepdims=True)

    diag = iota((leaves, coefs), 0) == iota((leaves, coefs), 1) // rank
    row_w = iota((leaves, width), 0)

    def apply(step, field, early):
        own_x[step] = field
        send(step, x_copy)
        xb = field.astype(BF16)
        full = nn(xb, up_w[...])
        masked = jnp.where(diag, full[:, 0:coefs], 0.0)
        part = masked[:, 0:LANES]
        for v in range(1, coefs // LANES):
            part = part + masked[:, v * LANES : (v + 1) * LANES]
        dup = part + pltpu.roll(part, rank, 1)
        rise = jnp.zeros((leaves, prank), F32)
        for i in range(leaves):
            rise = jnp.where(row == i, full[:, coefs + i * prank : coefs + (i + 1) * prank], rise)
        rise = rise + jnp.where(
            even, pltpu.roll(rise, leaves - 1, 0), pltpu.roll(rise, 1, 0)
        )
        own_ct[step, 0:leaves, :] = dup
        own_ct[step, leaves : 2 * leaves, :] = rise
        send(step, ct_copy)
        if early is not None:
            early()
        acc = 0.5 * field
        for i in range(leaves):
            acc = acc + jnp.where(row_w == i, nn(xb, near_t[i, 0]), 0.0)
        zero = jnp.zeros((leaves, LANES), F32)
        xs = pick_x(0, own_x.at[step], [[zero] * halves] * (n_near - 1))
        far, top = pick_ct(0, own_ct.at[step], [zero] * far_tiles, [zero] * n_top)
        receive(step, x_copy, 0)
        xs = pick_x(1, halo_x.at[step, 0], xs)
        receive(step, ct_copy, 0)
        far, top = pick_ct(1, halo_ct.at[step, 0], far, top)
        receive(step, x_copy, 1)
        xs = pick_x(2, halo_x.at[step, 1], xs)
        xs = [jnp.concatenate(x, 1).astype(BF16) for x in xs]

        def near_rows(acc, lo, hi):
            for i in range(lo, hi):
                r = nn(xs[0], near_t[i, 1])
                for k in range(2, n_near):
                    r = r + nn(xs[k - 1], near_t[i, k])
                acc = acc + jnp.where(row_w == i, r, 0.0)
            return acc

        acc = near_rows(acc, 0, leaves // 2)
        receive(step, ct_copy, 1)
        far, top = pick_ct(2, halo_ct.at[step, 1], far, top)
        lhs = jnp.concatenate(far + top, 1).astype(BF16)
        g = jnp.where(diag, nn(lhs, g_w[...]), 0.0).astype(BF16)
        acc = near_rows(acc, leaves // 2, leaves)
        return acc + nn(g, lb[...])

    def body(step, early):
        root = roots[0:1, 0:1]
        for s in range(1, steps):
            root = jnp.where(step == s, roots[0:1, s : s + 1], root)
        inverse = 1.0 / root
        prod = prod_buf[...]
        z = z_buf[...] + prod * inverse
        z_buf[...] = z
        last = step == steps - 1
        field = jnp.where(last, z, prod)
        image = apply(step, field, early)
        prod_buf[...] = jnp.where(last, image, prod - image * inverse)

    body(0, prepare)

    def loop(step, carry):
        body(step, None)
        return carry

    lax.fori_loop(1, steps, loop, 0)

    w = prod_buf[...]
    w_buf[...] = w
    proj = jnp.zeros((count, LANES), F32)
    for c in range(chunks):
        i, h = c // halves, c % halves
        proj = proj + bas[c * count : (c + 1) * count, :] * side_tile(w_buf, i, h * LANES)
    hcol = jnp.sum(proj, 1, keepdims=True)
    ww = jnp.sum(jnp.sum(w * w, 1, keepdims=True), 0, keepdims=True)
    at_h = count * count
    lane_c = iota((count, LANES), 1)
    row_c = iota((count, LANES), 0)
    lane1 = iota((1, LANES), 1)
    hsum = jnp.sum(jnp.where(lane_c == row_c + at_h, hcol, 0.0), 0, keepdims=True)
    slots[me] = gram_row[...] + hsum + jnp.where(lane1 == at_h + count, ww, 0.0)

    for target in others():
        pltpu.make_async_remote_copy(
            src_ref=slots.at[me],
            dst_ref=slots.at[me],
            send_sem=red_sem.at[0],
            recv_sem=red_sem.at[1],
            device_id=target,
            device_id_type=MESH,
        ).start()
    rest = pltpu.make_async_remote_copy(
        src_ref=slots.at[pl.ds(0, n_dev - 1)],
        dst_ref=slots.at[pl.ds(0, n_dev - 1)],
        send_sem=red_sem.at[0],
        recv_sem=red_sem.at[1],
        device_id=place(fast),
        device_id_type=MESH,
    )
    rest.wait_recv()
    total = jnp.sum(slots[...], 0) * (1.0 / (leaves * width * n_dev))
    hrow = jnp.where(lane1 < count, pltpu.roll(total, LANES - at_h, 1), 0.0)
    hcol = jnp.sum(jnp.where(lane_c == row_c, hrow, 0.0), 1, keepdims=True)
    gram = pltpu.roll(
        jnp.broadcast_to(total, (count, LANES)),
        LANES - count * (count - 1),
        1,
        stride=count,
        stride_axis=0,
    )
    quad = jnp.sum(hcol * (gram * hrow), 0, keepdims=True) - 2.0 * hrow * hrow
    quad = quad + jnp.where(lane1 == at_h + count, total, 0.0)
    squared = jnp.maximum(jnp.sum(quad, 1, keepdims=True), 0.0)
    beta = jnp.sqrt(squared + 1e-06)
    inverse = 1.0 / beta
    hess[...] = jnp.where(lane1 == count, beta, hrow)[:, 0 : count + 1]
    for h in range(halves):
        fit = jnp.zeros((leaves, LANES), F32)
        for j in range(count):
            vec = bas[pl.ds(j + count * h, leaves, stride=count * halves), :]
            fit = fit + hcol[j : j + 1, :] * vec
        part = w[:, h * LANES : (h + 1) * LANES]
        out[pl.ds(h, leaves, stride=halves), :] = (part - fit) * inverse
    rest.wait_send()

    def drain(step, carry):
        for make in (x_copy, ct_copy):
            make(step, 0).wait_send()

            @pl.when(has_slow)
            def _():
                make(step, 1).wait_send()

        return carry

    lax.fori_loop(0, steps, drain, 0)


def make_body(n_grp, n_leaf):
    def body(
        basis,
        roots,
        near_blocks,
        near_ids,
        leaf_basis,
        far_coupling,
        far_ids,
        transfer,
        top_coupling,
        top_ids,
    ):
        leaves, rank, width = leaf_basis.shape
        prank = transfer.shape[2]
        count = basis.shape[0]
        steps = roots.shape[0]
        n_near, n_far, n_top = near_ids.shape[1], far_ids.shape[1], top_ids.shape[1]
        n_dev = n_grp * n_leaf
        coefs = leaves * rank
        far_tiles = n_far * rank // LANES
        chunks = leaves * width // LANES
        vmem = pl.BlockSpec(memory_space=pltpu.VMEM)
        hbm = pl.BlockSpec(memory_space=pl.ANY)
        lb = leaf_basis.reshape(coefs, width)
        tr = transfer.reshape(coefs, prank)
        out, hess = pl.pallas_call(
            functools.partial(kernel, n_grp, n_leaf),
            out_shape=(
                jax.ShapeDtypeStruct((chunks, LANES), F32),
                jax.ShapeDtypeStruct((1, count + 1), F32),
            ),
            in_specs=[hbm] * 10,
            out_specs=(vmem, vmem),
            scratch_shapes=[
                pltpu.VMEM((chunks * count, LANES), F32),
                pltpu.VMEM((1, steps), F32),
                pltpu.VMEM(near_blocks.shape, BF16),
                pltpu.VMEM(near_blocks.shape, BF16),
                pltpu.VMEM(near_ids.shape, jnp.int32),
                pltpu.VMEM(lb.shape, BF16),
                pltpu.VMEM((width, coefs + leaves * prank), BF16),
                pltpu.VMEM(far_coupling.shape, BF16),
                pltpu.VMEM((coefs, n_far * rank), BF16),
                pltpu.VMEM(far_ids.shape, jnp.int32),
                pltpu.VMEM(tr.shape, BF16),
                pltpu.VMEM(top_coupling.shape, BF16),
                pltpu.VMEM(top_ids.shape, jnp.int32),
                pltpu.VMEM((n_far * rank + n_top * prank, coefs), BF16),
                pltpu.VMEM((3, n_near - 1, leaves, LANES), jnp.int32),
                pltpu.VMEM((3, far_tiles, leaves, LANES), jnp.int32),
                pltpu.VMEM((3, n_top, leaves, LANES), jnp.int32),
                pltpu.VMEM((steps, leaves, width), F32),
                pltpu.VMEM((steps, 2 * leaves, LANES), F32),
                pltpu.VMEM((steps, 2, leaves, width), F32),
                pltpu.VMEM((steps, 2, 2 * leaves, LANES), F32),
                pltpu.VMEM((leaves, width), F32),
                pltpu.VMEM((leaves, width), F32),
                pltpu.VMEM((leaves, width), F32),
                pltpu.VMEM((1, LANES), F32),
                pltpu.VMEM((n_dev, 1, LANES), F32),
                pltpu.SemaphoreType.DMA((9,)),
                pltpu.SemaphoreType.DMA((leaves,)),
                pltpu.SemaphoreType.DMA((steps, 2, 2)),
                pltpu.SemaphoreType.DMA((steps, 2, 2)),
                pltpu.SemaphoreType.DMA((2,)),
            ],
            compiler_params=pltpu.CompilerParams(
                collective_id=0, has_side_effects=True, vmem_limit_bytes=67043328
            ),
        )(
            basis,
            roots.reshape(1, steps),
            near_blocks,
            near_ids,
            lb,
            far_coupling,
            far_ids,
            tr,
            top_coupling,
            top_ids,
        )
        return out.reshape(leaves * width), hess.reshape(count + 1)

    return body


def solution(mesh):
    both = ("grp", "leaf")
    return jax.shard_map(
        make_body(mesh.shape["grp"], mesh.shape["leaf"]),
        mesh=mesh,
        in_specs=(
            P(None, both),
            P(),
            P(both, None, None, None),
            P(both, None),
            P(both, None, None),
            P(both, None, None, None),
            P(both, None),
            P(both, None, None),
            P(both, None, None, None),
            P(both, None),
        ),
        out_specs=(P(both), P()),
        check_vma=False,
    )
```

```python
import functools

import jax
import jax.numpy as jnp
from jax import lax
from jax.experimental import pallas as pl
from jax.experimental.pallas import tpu as pltpu
from jax.sharding import PartitionSpec as P

MESH = pl.DeviceIdType.MESH
F32 = jnp.float32
BF16 = jnp.bfloat16
LANES = 128


def nt(a, b):
    return lax.dot_general(a, b, (((1,), (1,)), ((), ())), preferred_element_type=F32)


def nn(a, b):
    return lax.dot_general(a, b, (((1,), (0,)), ((), ())), preferred_element_type=F32)


def iota(shape, dim):
    return lax.broadcasted_iota(jnp.int32, shape, dim)


def kernel(
    n_grp,
    n_leaf,
    basis_hbm,
    roots_hbm,
    near_hbm,
    near_ids_hbm,
    lb_hbm,
    fc_hbm,
    far_ids_hbm,
    tr_hbm,
    tc_hbm,
    top_ids_hbm,
    out,
    hess,
    bas,
    roots,
    near,
    near_t,
    near_ids,
    lb,
    up_w,
    fc,
    fcc,
    far_ids,
    tr,
    tc,
    top_ids,
    g_w,
    near_ix,
    far_ix,
    top_ix,
    own_x,
    own_ct,
    halo_x,
    halo_ct,
    prod_buf,
    z_buf,
    w_buf,
    gram_row,
    slots,
    load_sem,
    near_sem,
    send_sem,
    recv_sem,
    red_sem,
    ready_sem,
):
    n_dev = n_grp * n_leaf
    rounds = ready_sem.shape[0]
    leaves, n_near, width, _ = near.shape
    n_far, rank = fc.shape[1], fc.shape[2]
    n_top, prank = tc.shape[1], tc.shape[2]
    parents = tc.shape[0]
    count = basis_hbm.shape[0]
    steps = roots.shape[1]
    coefs = leaves * rank
    halves = width // LANES
    chunks = leaves * halves
    far_tiles = n_far * rank // LANES
    mg, ml = lax.axis_index("grp"), lax.axis_index("leaf")
    me = mg * n_leaf + ml

    def place(index):
        return (lax.div(index, n_leaf), lax.rem(index, n_leaf))

    odd = lax.rem(me, 2)
    fast = me + 1 - 2 * odd
    slow = me - 1 + 2 * odd
    has_slow = jnp.logical_and(slow >= 0, slow < n_dev)

    def others():
        for dg in range(n_grp):
            g = lax.rem(mg + dg, n_grp)
            for dl in range(n_leaf):
                if dg or dl:
                    yield (g, lax.rem(ml + dl, n_leaf))

    first = [
        pltpu.make_async_copy(
            basis_hbm.at[:, c * LANES : (c + 1) * LANES],
            bas.at[c * count : (c + 1) * count, :],
            load_sem.at[0],
        )
        for c in range(chunks)
    ]
    all_basis = pltpu.make_async_copy(bas, bas, load_sem.at[0])
    loads = [
        pltpu.make_async_copy(src, dst, load_sem.at[1 + n])
        for n, (src, dst) in enumerate(
            (
                (roots_hbm, roots),
                (near_ids_hbm, near_ids),
                (far_ids_hbm, far_ids),
                (top_ids_hbm, top_ids),
                (lb_hbm, lb),
                (tr_hbm, tr),
                (fc_hbm, fc),
                (tc_hbm, tc),
            )
        )
    ]
    lb_copy, tr_copy, fc_copy, tc_copy = loads[4:]
    for copy in first + loads:
        copy.start()
    for i in range(leaves):
        pltpu.make_async_copy(near_hbm.at[i], near.at[i], near_sem.at[i]).start()

    barrier = pltpu.get_barrier_semaphore()

    def around(distance, call):
        for other in (me - distance, me + distance):

            @pl.when(jnp.logical_and(other >= 0, other < n_dev))
            def _():
                call(other)

    def signal(sem, distance):
        def one(other):
            pl.semaphore_signal(sem, inc=1, device_id=place(other), device_id_type=MESH)

        around(distance, one)

    def await_signals(sem, distance):
        peers = jnp.where(me >= distance, 1, 0) + jnp.where(me + distance < n_dev, 1, 0)
        pl.semaphore_wait(sem, peers)

    signal(barrier, 1)

    row = iota((leaves, LANES), 0)
    lane = iota((leaves, LANES), 1)
    low = lane < rank
    even = row % 2 == 0
    own_base = me * leaves
    shift = (1 - 2 * odd) * leaves

    def side_tile(source, j, lo):
        return jnp.broadcast_to(source[j : j + 1, lo : lo + LANES], (leaves, LANES))

    @pl.when(jnp.logical_not(has_slow))
    def _():
        for step in range(steps):
            halo_x[step, 1] = jnp.zeros((leaves, width), F32)
            halo_ct[step, 1] = jnp.zeros((2 * leaves, LANES), F32)

    for copy in loads[:4]:
        copy.wait()
    nid = near_ids[...] - own_base
    for k in range(1, n_near):
        tile = jnp.broadcast_to(nid[:, k : k + 1], (leaves, LANES))
        near_ix[0, k - 1] = tile
        near_ix[1, k - 1] = tile - shift
        near_ix[2, k - 1] = tile + shift
    fid = far_ids[...] - own_base
    for v in range(far_tiles):
        tile = jnp.where(low, fid[:, 2 * v : 2 * v + 1], fid[:, 2 * v + 1 : 2 * v + 2])
        far_ix[0, v] = tile
        far_ix[1, v] = tile - shift
        far_ix[2, v] = tile + shift
    tid = jnp.zeros((leaves, n_top), jnp.int32)
    for p in range(parents):
        tid = jnp.where(iota((leaves, n_top), 0) // 2 == p, top_ids[p : p + 1, :], tid)
    tid = (tid - me * parents) * 2
    for k in range(n_top):
        tile = jnp.broadcast_to(tid[:, k : k + 1], (leaves, LANES))
        top_ix[0, k] = tile
        top_ix[1, k] = tile - shift
        top_ix[2, k] = tile + shift

    all_basis.wait()
    for h in range(halves):
        prod_buf[:, h * LANES : (h + 1) * LANES] = bas[
            pl.ds(count - 1 + count * h, leaves, stride=count * halves), :
        ]
    z_buf[...] = jnp.zeros_like(z_buf)

    lb_copy.wait()
    lb_t = lb[...].T
    up_w[:, 0:coefs] = lb_t
    tr_copy.wait()
    for i in range(leaves):
        block = nn(lb_t[:, i * rank : (i + 1) * rank], tr[i * rank : (i + 1) * rank, :])
        up_w[:, coefs + i * prank : coefs + (i + 1) * prank] = block.astype(BF16)

    await_signals(barrier, 1)

    def x_copy(step, side):
        return pltpu.make_async_remote_copy(
            src_ref=own_x.at[step],
            dst_ref=halo_x.at[step, side],
            send_sem=send_sem.at[step, 0, side],
            recv_sem=recv_sem.at[step, 0, side],
            device_id=place((fast, slow)[side]),
            device_id_type=MESH,
        )

    def ct_copy(step, side):
        return pltpu.make_async_remote_copy(
            src_ref=own_ct.at[step],
            dst_ref=halo_ct.at[step, side],
            send_sem=send_sem.at[step, 1, side],
            recv_sem=recv_sem.at[step, 1, side],
            device_id=place((fast, slow)[side]),
            device_id_type=MESH,
        )

    def send(step, make):
        @pl.when(has_slow)
        def _():
            make(step, 1).start()

        make(step, 0).start()

    def receive(step, make, side):
        if side == 0:
            make(step, 0).wait_recv()
        else:

            @pl.when(has_slow)
            def _():
                make(step, 1).wait_recv()

    def pick_x(ix, source, acc):
        out = [list(a) for a in acc]
        rows = [[side_tile(source, j, h * LANES) for h in range(halves)] for j in range(leaves)]
        for k in range(n_near - 1):
            index = near_ix[ix, k]
            for j in range(leaves):
                hit = index == j
                for h in range(halves):
                    out[k][h] = jnp.where(hit, rows[j][h], out[k][h])
        return out

    def pick_ct(ix, source, far, top):
        far, top = list(far), list(top)
        for j in range(leaves):
            tile = side_tile(source, j, 0)
            for v in range(far_tiles):
                far[v] = jnp.where(far_ix[ix, v] == j, tile, far[v])
        for j in range(0, leaves, 2):
            tile = side_tile(source, leaves + j, 0)
            for k in range(n_top):
                top[k] = jnp.where(top_ix[ix, k] == j, tile, top[k])
        return far, top

    def prepare():
        def turn(i, carry):
            pltpu.make_async_copy(near_hbm.at[i], near.at[i], near_sem.at[i]).wait()
            for k in range(n_near):
                near_t[i, k] = near[i, k].T
            return carry

        lax.fori_loop(0, leaves, turn, 0)
        fc_copy.wait()
        for k in range(n_far):
            for i in range(leaves):
                fcc[i * rank : (i + 1) * rank, k * rank : (k + 1) * rank] = fc[i, k]
        g_w[0 : n_far * rank, :] = fcc[...].T
        tc_copy.wait()
        base = n_far * rank

        def fold(k, carry):
            start = pl.multiple_of(base + k * prank, prank)
            for p in range(parents):
                pair = tr[p * 2 * rank : (p + 1) * 2 * rank, :]
                block = nn(pair, tc[p, k]).astype(BF16).T
                g_w[pl.ds(start, prank), p * 2 * rank : (p + 1) * 2 * rank] = block
            return carry

        lax.fori_loop(0, n_top, fold, 0)
        flat = jnp.concatenate(
            [bas[c * count : (c + 1) * count, :] for c in range(chunks)], 1
        )
        gram = lax.dot_general(
            flat,
            flat,
            (((1,), (1,)), ((), ())),
            precision=lax.Precision.HIGHEST,
            preferred_element_type=F32,
        )
        flip = iota((count, count), 0) + iota((count, count), 1) == count - 1
        gram = lax.dot_general(
            flip.astype(F32),
            gram,
            (((1,), (0,)), ((), ())),
            precision=lax.Precision.HIGHEST,
            preferred_element_type=F32,
        )
        gram = jnp.pad(gram, ((0, 0), (0, LANES - count)))
        spread = pltpu.roll(gram, 0, 1, stride=count, stride_axis=0)
        gram_row[...] = jnp.sum(spread, 0, keepdims=True)

    diag = iota((leaves, coefs), 0) == iota((leaves, coefs), 1) // rank
    row_w = iota((leaves, width), 0)

    def greet(step, distance):
        @pl.when(step >= 2)
        def _():
            await_signals(ready_sem.at[step - 1], distance // 2)

        signal(ready_sem.at[step], distance)

    def apply(step, field, early, distance):
        own_x[step] = field
        send(step, x_copy)
        xb = field.astype(BF16)
        full = nn(xb, up_w[...])
        masked = jnp.where(diag, full[:, 0:coefs], 0.0)
        part = masked[:, 0:LANES]
        for v in range(1, coefs // LANES):
            part = part + masked[:, v * LANES : (v + 1) * LANES]
        dup = part + pltpu.roll(part, rank, 1)
        rise = jnp.zeros((leaves, prank), F32)
        for i in range(leaves):
            rise = jnp.where(row == i, full[:, coefs + i * prank : coefs + (i + 1) * prank], rise)
        rise = rise + jnp.where(
            even, pltpu.roll(rise, leaves - 1, 0), pltpu.roll(rise, 1, 0)
        )
        own_ct[step, 0:leaves, :] = dup
        own_ct[step, leaves : 2 * leaves, :] = rise
        send(step, ct_copy)
        if early is not None:
            early()
        else:
            greet(step, distance)
        acc = 0.5 * field
        for i in range(leaves):
            acc = acc + jnp.where(row_w == i, nn(xb, near_t[i, 0]), 0.0)
        zero = jnp.zeros((leaves, LANES), F32)
        xs = pick_x(0, own_x.at[step], [[zero] * halves] * (n_near - 1))
        far, top = pick_ct(0, own_ct.at[step], [zero] * far_tiles, [zero] * n_top)
        receive(step, x_copy, 0)
        xs = pick_x(1, halo_x.at[step, 0], xs)
        receive(step, ct_copy, 0)
        far, top = pick_ct(1, halo_ct.at[step, 0], far, top)
        receive(step, x_copy, 1)
        xs = pick_x(2, halo_x.at[step, 1], xs)
        xs = [jnp.concatenate(x, 1).astype(BF16) for x in xs]

        def near_rows(acc, lo, hi):
            for i in range(lo, hi):
                r = nn(xs[0], near_t[i, 1])
                for k in range(2, n_near):
                    r = r + nn(xs[k - 1], near_t[i, k])
                acc = acc + jnp.where(row_w == i, r, 0.0)
            return acc

        acc = near_rows(acc, 0, leaves // 2)
        receive(step, ct_copy, 1)
        far, top = pick_ct(2, halo_ct.at[step, 1], far, top)
        lhs = jnp.concatenate(far + top, 1).astype(BF16)
        g = jnp.where(diag, nn(lhs, g_w[...]), 0.0).astype(BF16)
        acc = near_rows(acc, leaves // 2, leaves)
        return acc + nn(g, lb[...])

    def body(step, early, distance):
        root = roots[0:1, 0:1]
        for s in range(1, steps):
            root = jnp.where(step == s, roots[0:1, s : s + 1], root)
        inverse = 1.0 / root
        prod = prod_buf[...]
        z = z_buf[...] + prod * inverse
        z_buf[...] = z
        last = step == steps - 1
        field = jnp.where(last, z, prod)
        image = apply(step, field, early, distance)
        prod_buf[...] = jnp.where(last, image, prod - image * inverse)

    body(0, prepare, 1)

    def loop(step, distance):
        body(step, None, distance)
        return distance * 2

    lax.fori_loop(1, steps, loop, 2)
    await_signals(ready_sem.at[steps - 1], 2 ** (steps - 1))
    for r in range(steps, rounds):
        signal(ready_sem.at[r], 2**r)
        await_signals(ready_sem.at[r], 2**r)

    w = prod_buf[...]
    w_buf[...] = w
    proj = jnp.zeros((count, LANES), F32)
    for c in range(chunks):
        i, h = c // halves, c % halves
        proj = proj + bas[c * count : (c + 1) * count, :] * side_tile(w_buf, i, h * LANES)
    hcol = jnp.sum(proj, 1, keepdims=True)
    ww = jnp.sum(jnp.sum(w * w, 1, keepdims=True), 0, keepdims=True)
    at_h = count * count
    lane_c = iota((count, LANES), 1)
    row_c = iota((count, LANES), 0)
    lane1 = iota((1, LANES), 1)
    hsum = jnp.sum(jnp.where(lane_c == row_c + at_h, hcol, 0.0), 0, keepdims=True)
    slots[me] = gram_row[...] + hsum + jnp.where(lane1 == at_h + count, ww, 0.0)

    for target in others():
        pltpu.make_async_remote_copy(
            src_ref=slots.at[me],
            dst_ref=slots.at[me],
            send_sem=red_sem.at[0],
            recv_sem=red_sem.at[1],
            device_id=target,
            device_id_type=MESH,
        ).start()
    rest = pltpu.make_async_remote_copy(
        src_ref=slots.at[pl.ds(0, n_dev - 1)],
        dst_ref=slots.at[pl.ds(0, n_dev - 1)],
        send_sem=red_sem.at[0],
        recv_sem=red_sem.at[1],
        device_id=place(fast),
        device_id_type=MESH,
    )
    rest.wait_recv()
    total = jnp.sum(slots[...], 0) * (1.0 / (leaves * width * n_dev))
    hrow = jnp.where(lane1 < count, pltpu.roll(total, LANES - at_h, 1), 0.0)
    hcol = jnp.sum(jnp.where(lane_c == row_c, hrow, 0.0), 1, keepdims=True)
    gram = pltpu.roll(
        jnp.broadcast_to(total, (count, LANES)),
        LANES - count * (count - 1),
        1,
        stride=count,
        stride_axis=0,
    )
    quad = jnp.sum(hcol * (gram * hrow), 0, keepdims=True) - 2.0 * hrow * hrow
    quad = quad + jnp.where(lane1 == at_h + count, total, 0.0)
    squared = jnp.maximum(jnp.sum(quad, 1, keepdims=True), 0.0)
    beta = jnp.sqrt(squared + 1e-06)
    inverse = 1.0 / beta
    hess[...] = jnp.where(lane1 == count, beta, hrow)[:, 0 : count + 1]
    for h in range(halves):
        fit = jnp.zeros((leaves, LANES), F32)
        for j in range(count):
            vec = bas[pl.ds(j + count * h, leaves, stride=count * halves), :]
            fit = fit + hcol[j : j + 1, :] * vec
        part = w[:, h * LANES : (h + 1) * LANES]
        out[pl.ds(h, leaves, stride=halves), :] = (part - fit) * inverse
    rest.wait_send()

    def drain(step, carry):
        for make in (x_copy, ct_copy):
            make(step, 0).wait_send()

            @pl.when(has_slow)
            def _():
                make(step, 1).wait_send()

        return carry

    lax.fori_loop(0, steps, drain, 0)


def make_body(n_grp, n_leaf):
    def body(
        basis,
        roots,
        near_blocks,
        near_ids,
        leaf_basis,
        far_coupling,
        far_ids,
        transfer,
        top_coupling,
        top_ids,
    ):
        leaves, rank, width = leaf_basis.shape
        prank = transfer.shape[2]
        count = basis.shape[0]
        steps = roots.shape[0]
        n_near, n_far, n_top = near_ids.shape[1], far_ids.shape[1], top_ids.shape[1]
        n_dev = n_grp * n_leaf
        coefs = leaves * rank
        far_tiles = n_far * rank // LANES
        chunks = leaves * width // LANES
        vmem = pl.BlockSpec(memory_space=pltpu.VMEM)
        hbm = pl.BlockSpec(memory_space=pl.ANY)
        lb = leaf_basis.reshape(coefs, width)
        tr = transfer.reshape(coefs, prank)
        out, hess = pl.pallas_call(
            functools.partial(kernel, n_grp, n_leaf),
            out_shape=(
                jax.ShapeDtypeStruct((chunks, LANES), F32),
                jax.ShapeDtypeStruct((1, count + 1), F32),
            ),
            in_specs=[hbm] * 10,
            out_specs=(vmem, vmem),
            scratch_shapes=[
                pltpu.VMEM((chunks * count, LANES), F32),
                pltpu.VMEM((1, steps), F32),
                pltpu.VMEM(near_blocks.shape, BF16),
                pltpu.VMEM(near_blocks.shape, BF16),
                pltpu.VMEM(near_ids.shape, jnp.int32),
                pltpu.VMEM(lb.shape, BF16),
                pltpu.VMEM((width, coefs + leaves * prank), BF16),
                pltpu.VMEM(far_coupling.shape, BF16),
                pltpu.VMEM((coefs, n_far * rank), BF16),
                pltpu.VMEM(far_ids.shape, jnp.int32),
                pltpu.VMEM(tr.shape, BF16),
                pltpu.VMEM(top_coupling.shape, BF16),
                pltpu.VMEM(top_ids.shape, jnp.int32),
                pltpu.VMEM((n_far * rank + n_top * prank, coefs), BF16),
                pltpu.VMEM((3, n_near - 1, leaves, LANES), jnp.int32),
                pltpu.VMEM((3, far_tiles, leaves, LANES), jnp.int32),
                pltpu.VMEM((3, n_top, leaves, LANES), jnp.int32),
                pltpu.VMEM((steps, leaves, width), F32),
                pltpu.VMEM((steps, 2 * leaves, LANES), F32),
                pltpu.VMEM((steps, 2, leaves, width), F32),
                pltpu.VMEM((steps, 2, 2 * leaves, LANES), F32),
                pltpu.VMEM((leaves, width), F32),
                pltpu.VMEM((leaves, width), F32),
                pltpu.VMEM((leaves, width), F32),
                pltpu.VMEM((1, LANES), F32),
                pltpu.VMEM((n_dev, 1, LANES), F32),
                pltpu.SemaphoreType.DMA((9,)),
                pltpu.SemaphoreType.DMA((leaves,)),
                pltpu.SemaphoreType.DMA((steps, 2, 2)),
                pltpu.SemaphoreType.DMA((steps, 2, 2)),
                pltpu.SemaphoreType.DMA((2,)),
                pltpu.SemaphoreType.REGULAR((max(steps, (n_dev - 1).bit_length()),)),
            ],
            compiler_params=pltpu.CompilerParams(
                collective_id=0, has_side_effects=True, vmem_limit_bytes=48 * 1024 * 1024
            ),
        )(
            *(
                pltpu.with_memory_space_constraint(operand, pltpu.HBM)
                for operand in (
                    basis,
                    roots.reshape(1, steps),
                    near_blocks,
                    near_ids,
                    lb,
                    far_coupling,
                    far_ids,
                    tr,
                    top_coupling,
                    top_ids,
                )
            )
        )
        return out.reshape(leaves * width), hess.reshape(count + 1)

    return body


def solution(mesh):
    both = ("grp", "leaf")
    return jax.shard_map(
        make_body(mesh.shape["grp"], mesh.shape["leaf"]),
        mesh=mesh,
        in_specs=(
            P(None, both),
            P(),
            P(both, None, None, None),
            P(both, None),
            P(both, None, None),
            P(both, None, None, None),
            P(both, None),
            P(both, None, None),
            P(both, None, None, None),
            P(both, None),
        ),
        out_specs=(P(both), P()),
        check_vma=False,
    )
```

```python
import functools

import jax
import jax.numpy as jnp
from jax import lax
from jax.experimental import pallas as pl
from jax.experimental.pallas import tpu as pltpu
from jax.sharding import PartitionSpec as P

MESH = pl.DeviceIdType.MESH
F32 = jnp.float32
BF16 = jnp.bfloat16
LANES = 128


def nt(a, b):
    return lax.dot_general(a, b, (((1,), (1,)), ((), ())), preferred_element_type=F32)


def nn(a, b):
    return lax.dot_general(a, b, (((1,), (0,)), ((), ())), preferred_element_type=F32)


def iota(shape, dim):
    return lax.broadcasted_iota(jnp.int32, shape, dim)


def kernel(
    n_grp,
    n_leaf,
    basis_hbm,
    roots_hbm,
    near_hbm,
    near_ids_hbm,
    lb_hbm,
    fc_hbm,
    far_ids_hbm,
    tr_hbm,
    tc_hbm,
    top_ids_hbm,
    out,
    hess,
    bas,
    roots,
    near,
    near_t,
    near_ids,
    lb,
    up_w,
    fc,
    fcc,
    far_ids,
    tr,
    tc,
    top_ids,
    g_w,
    near_ix,
    far_ix,
    top_ix,
    own_x,
    own_ct,
    halo_x,
    halo_ct,
    prod_buf,
    z_buf,
    w_buf,
    gram_row,
    slots,
    load_sem,
    near_sem,
    send_sem,
    recv_sem,
    red_sem,
    ready_sem,
):
    n_dev = n_grp * n_leaf
    rounds = ready_sem.shape[0]
    leaves, n_near, width, _ = near.shape
    n_far, rank = fc.shape[1], fc.shape[2]
    n_top, prank = tc.shape[1], tc.shape[2]
    parents = tc.shape[0]
    count = basis_hbm.shape[0]
    steps = roots.shape[1]
    coefs = leaves * rank
    halves = width // LANES
    chunks = leaves * halves
    far_tiles = n_far * rank // LANES
    mg, ml = lax.axis_index("grp"), lax.axis_index("leaf")
    me = mg * n_leaf + ml

    def place(index):
        return (lax.div(index, n_leaf), lax.rem(index, n_leaf))

    odd = lax.rem(me, 2)
    fast = me + 1 - 2 * odd
    slow = me - 1 + 2 * odd
    has_slow = jnp.logical_and(slow >= 0, slow < n_dev)

    def others():
        for dg in range(n_grp):
            g = lax.rem(mg + dg, n_grp)
            for dl in range(n_leaf):
                if dg or dl:
                    yield (g, lax.rem(ml + dl, n_leaf))

    first = [
        pltpu.make_async_copy(
            basis_hbm.at[:, c * LANES : (c + 1) * LANES],
            bas.at[c * count : (c + 1) * count, :],
            load_sem.at[0],
        )
        for c in range(chunks)
    ]
    all_basis = pltpu.make_async_copy(bas, bas, load_sem.at[0])
    loads = [
        pltpu.make_async_copy(src, dst, load_sem.at[1 + n])
        for n, (src, dst) in enumerate(
            (
                (roots_hbm, roots),
                (near_ids_hbm, near_ids),
                (far_ids_hbm, far_ids),
                (top_ids_hbm, top_ids),
                (lb_hbm, lb),
                (tr_hbm, tr),
                (fc_hbm, fc),
                (tc_hbm, tc),
            )
        )
    ]
    lb_copy, tr_copy, fc_copy, tc_copy = loads[4:]
    for copy in first + loads:
        copy.start()
    for i in range(leaves):
        pltpu.make_async_copy(near_hbm.at[i], near.at[i], near_sem.at[i]).start()

    barrier = pltpu.get_barrier_semaphore()

    def around(distance, call):
        for other in (me - distance, me + distance):

            @pl.when(jnp.logical_and(other >= 0, other < n_dev))
            def _():
                call(other)

    def signal(sem, distance):
        def one(other):
            pl.semaphore_signal(sem, inc=1, device_id=place(other), device_id_type=MESH)

        around(distance, one)

    def await_signals(sem, distance):
        peers = jnp.where(me >= distance, 1, 0) + jnp.where(me + distance < n_dev, 1, 0)
        pl.semaphore_wait(sem, peers)

    signal(barrier, 1)

    row = iota((leaves, LANES), 0)
    lane = iota((leaves, LANES), 1)
    low = lane < rank
    even = row % 2 == 0
    own_base = me * leaves
    shift = (1 - 2 * odd) * leaves

    def side_tile(source, j, lo):
        return jnp.broadcast_to(source[j : j + 1, lo : lo + LANES], (leaves, LANES))

    @pl.when(jnp.logical_not(has_slow))
    def _():
        for step in range(steps):
            halo_x[step, 1] = jnp.zeros((leaves, width), F32)
            halo_ct[step, 1] = jnp.zeros((2 * leaves, LANES), F32)

    for copy in loads[:4]:
        copy.wait()
    nid = near_ids[...] - own_base
    for k in range(1, n_near):
        tile = jnp.broadcast_to(nid[:, k : k + 1], (leaves, LANES))
        near_ix[0, k - 1] = tile
        near_ix[1, k - 1] = tile - shift
        near_ix[2, k - 1] = tile + shift
    fid = far_ids[...] - own_base
    for v in range(far_tiles):
        tile = jnp.where(low, fid[:, 2 * v : 2 * v + 1], fid[:, 2 * v + 1 : 2 * v + 2])
        far_ix[0, v] = tile
        far_ix[1, v] = tile - shift
        far_ix[2, v] = tile + shift
    tid = jnp.zeros((leaves, n_top), jnp.int32)
    for p in range(parents):
        tid = jnp.where(iota((leaves, n_top), 0) // 2 == p, top_ids[p : p + 1, :], tid)
    tid = (tid - me * parents) * 2
    for k in range(n_top):
        tile = jnp.broadcast_to(tid[:, k : k + 1], (leaves, LANES))
        top_ix[0, k] = tile
        top_ix[1, k] = tile - shift
        top_ix[2, k] = tile + shift

    all_basis.wait()
    for h in range(halves):
        prod_buf[:, h * LANES : (h + 1) * LANES] = bas[
            pl.ds(count - 1 + count * h, leaves, stride=count * halves), :
        ]
    z_buf[...] = jnp.zeros_like(z_buf)

    lb_copy.wait()
    up_w[...] = lb[...].T
    tr_copy.wait()

    await_signals(barrier, 1)

    def x_copy(step, side):
        return pltpu.make_async_remote_copy(
            src_ref=own_x.at[step],
            dst_ref=halo_x.at[step, side],
            send_sem=send_sem.at[step, 0, side],
            recv_sem=recv_sem.at[step, 0, side],
            device_id=place((fast, slow)[side]),
            device_id_type=MESH,
        )

    def ct_copy(step, side):
        return pltpu.make_async_remote_copy(
            src_ref=own_ct.at[step],
            dst_ref=halo_ct.at[step, side],
            send_sem=send_sem.at[step, 1, side],
            recv_sem=recv_sem.at[step, 1, side],
            device_id=place((fast, slow)[side]),
            device_id_type=MESH,
        )

    def send(step, make):
        @pl.when(has_slow)
        def _():
            make(step, 1).start()

        make(step, 0).start()

    def receive(step, make, side):
        if side == 0:
            make(step, 0).wait_recv()
        else:

            @pl.when(has_slow)
            def _():
                make(step, 1).wait_recv()

    def pick_x(ix, source, acc):
        out = [list(a) for a in acc]
        rows = [[side_tile(source, j, h * LANES) for h in range(halves)] for j in range(leaves)]
        for k in range(n_near - 1):
            index = near_ix[ix, k]
            for j in range(leaves):
                hit = index == j
                for h in range(halves):
                    out[k][h] = jnp.where(hit, rows[j][h], out[k][h])
        return out

    def pick_ct(ix, source, far, top):
        far, top = list(far), list(top)
        for j in range(leaves):
            tile = side_tile(source, j, 0)
            for v in range(far_tiles):
                far[v] = jnp.where(far_ix[ix, v] == j, tile, far[v])
        for j in range(0, leaves, 2):
            tile = side_tile(source, leaves + j, 0)
            for k in range(n_top):
                top[k] = jnp.where(top_ix[ix, k] == j, tile, top[k])
        return far, top

    def prepare():
        base = n_far * rank
        fc_copy.wait()
        tc_copy.wait()

        def fold(k):
            start = pl.multiple_of(base + k * prank, prank)
            for p in range(parents):
                pair = tr[p * 2 * rank : (p + 1) * 2 * rank, :]
                block = nn(pair, tc[p, k]).astype(BF16).T
                g_w[pl.ds(start, prank), p * 2 * rank : (p + 1) * 2 * rank] = block

        def turn(i, carry):
            pltpu.make_async_copy(near_hbm.at[i], near.at[i], near_sem.at[i]).wait()
            start = pl.multiple_of(i * rank, rank)
            for k in range(n_far):
                fcc[pl.ds(start, rank), k * rank : (k + 1) * rank] = fc[i, k]
            if n_top == leaves:
                fold(i)
            for k in range(1, n_near):
                near_t[i, k - 1] = near[i, k].T
            return carry

        lax.fori_loop(0, leaves, turn, 0)
        if n_top != leaves:
            for k in range(n_top):
                fold(k)
        g_w[0:base, :] = fcc[...].T

    def make_gram():
        flat = jnp.concatenate(
            [bas[c * count : (c + 1) * count, :] for c in range(chunks)], 1
        )
        gram = lax.dot_general(
            flat,
            flat,
            (((1,), (1,)), ((), ())),
            precision=lax.Precision.HIGHEST,
            preferred_element_type=F32,
        )
        flip = iota((count, count), 0) + iota((count, count), 1) == count - 1
        gram = lax.dot_general(
            flip.astype(F32),
            gram,
            (((1,), (0,)), ((), ())),
            precision=lax.Precision.HIGHEST,
            preferred_element_type=F32,
        )
        gram = jnp.pad(gram, ((0, 0), (0, LANES - count)))
        spread = pltpu.roll(gram, 0, 1, stride=count, stride_axis=0)
        gram_row[...] = jnp.sum(spread, 0, keepdims=True)

    diag = iota((leaves, coefs), 0) == iota((leaves, coefs), 1) // rank
    row_w = iota((leaves, width), 0)

    def greet(step, distance):
        @pl.when(step >= 2)
        def _():
            await_signals(ready_sem.at[step - 1], distance // 2)

        signal(ready_sem.at[step], distance)
        pl.when(step == 1)(make_gram)

    def apply(step, field, early, distance):
        own_x[step] = field
        send(step, x_copy)
        xb = field.astype(BF16)
        masked = jnp.where(diag, nn(xb, up_w[...]), 0.0)
        part = masked[:, 0:LANES]
        for v in range(1, coefs // LANES):
            part = part + masked[:, v * LANES : (v + 1) * LANES]
        dup = part + pltpu.roll(part, rank, 1)
        rise = nn(masked.astype(BF16), tr[...])
        rise = rise + jnp.where(
            even, pltpu.roll(rise, leaves - 1, 0), pltpu.roll(rise, 1, 0)
        )
        own_ct[step, 0:leaves, :] = dup
        own_ct[step, leaves : 2 * leaves, :] = rise
        send(step, ct_copy)
        if early is not None:
            early()
        else:
            greet(step, distance)
        acc = 0.5 * field
        for i in range(leaves):
            acc = acc + jnp.where(row_w == i, nt(xb, near[i, 0]), 0.0)
        zero = jnp.zeros((leaves, LANES), F32)
        xs = pick_x(0, own_x.at[step], [[zero] * halves] * (n_near - 1))
        far, top = pick_ct(0, own_ct.at[step], [zero] * far_tiles, [zero] * n_top)
        receive(step, x_copy, 0)
        xs = pick_x(1, halo_x.at[step, 0], xs)
        receive(step, ct_copy, 0)
        far, top = pick_ct(1, halo_ct.at[step, 0], far, top)
        receive(step, x_copy, 1)
        xs = pick_x(2, halo_x.at[step, 1], xs)
        xs = [jnp.concatenate(x, 1).astype(BF16) for x in xs]

        def near_rows(acc, lo, hi):
            for i in range(lo, hi):
                r = nn(xs[0], near_t[i, 0])
                for k in range(1, n_near - 1):
                    r = r + nn(xs[k], near_t[i, k])
                acc = acc + jnp.where(row_w == i, r, 0.0)
            return acc

        acc = near_rows(acc, 0, leaves // 2)
        receive(step, ct_copy, 1)
        far, top = pick_ct(2, halo_ct.at[step, 1], far, top)
        lhs = jnp.concatenate(far + top, 1).astype(BF16)
        g = jnp.where(diag, nn(lhs, g_w[...]), 0.0).astype(BF16)
        acc = near_rows(acc, leaves // 2, leaves)
        return acc + nn(g, lb[...])

    def body(step, early, distance):
        root = roots[0:1, 0:1]
        for s in range(1, steps):
            root = jnp.where(step == s, roots[0:1, s : s + 1], root)
        inverse = 1.0 / root
        prod = prod_buf[...]
        z = z_buf[...] + prod * inverse
        z_buf[...] = z
        last = step == steps - 1
        field = jnp.where(last, z, prod)
        image = apply(step, field, early, distance)
        prod_buf[...] = jnp.where(last, image, prod - image * inverse)

    body(0, prepare, 1)

    def loop(step, distance):
        body(step, None, distance)
        return distance * 2

    lax.fori_loop(1, steps, loop, 2)
    await_signals(ready_sem.at[steps - 1], 2 ** (steps - 1))
    for r in range(steps, rounds):
        signal(ready_sem.at[r], 2**r)
        await_signals(ready_sem.at[r], 2**r)

    w = prod_buf[...]
    w_buf[...] = w
    proj = jnp.zeros((count, LANES), F32)
    for c in range(chunks):
        i, h = c // halves, c % halves
        proj = proj + bas[c * count : (c + 1) * count, :] * side_tile(w_buf, i, h * LANES)
    hcol = jnp.sum(proj, 1, keepdims=True)
    ww = jnp.sum(jnp.sum(w * w, 1, keepdims=True), 0, keepdims=True)
    at_h = count * count
    lane_c = iota((count, LANES), 1)
    row_c = iota((count, LANES), 0)
    lane1 = iota((1, LANES), 1)
    hsum = jnp.sum(jnp.where(lane_c == row_c + at_h, hcol, 0.0), 0, keepdims=True)
    slots[me] = gram_row[...] + hsum + jnp.where(lane1 == at_h + count, ww, 0.0)

    for target in others():
        pltpu.make_async_remote_copy(
            src_ref=slots.at[me],
            dst_ref=slots.at[me],
            send_sem=red_sem.at[0],
            recv_sem=red_sem.at[1],
            device_id=target,
            device_id_type=MESH,
        ).start()
    rest = pltpu.make_async_remote_copy(
        src_ref=slots.at[pl.ds(0, n_dev - 1)],
        dst_ref=slots.at[pl.ds(0, n_dev - 1)],
        send_sem=red_sem.at[0],
        recv_sem=red_sem.at[1],
        device_id=place(fast),
        device_id_type=MESH,
    )
    def drain(step, carry):
        for make in (x_copy, ct_copy):
            make(step, 0).wait_send()

            @pl.when(has_slow)
            def _():
                make(step, 1).wait_send()

        return carry

    lax.fori_loop(0, steps, drain, 0)
    rest.wait_recv()
    total = jnp.sum(slots[...], 0) * (1.0 / (leaves * width * n_dev))
    hrow = jnp.where(lane1 < count, pltpu.roll(total, LANES - at_h, 1), 0.0)
    hcol = jnp.sum(jnp.where(lane_c == row_c, hrow, 0.0), 1, keepdims=True)
    gram = pltpu.roll(
        jnp.broadcast_to(total, (count, LANES)),
        LANES - count * (count - 1),
        1,
        stride=count,
        stride_axis=0,
    )
    quad = jnp.sum(hcol * (gram * hrow), 0, keepdims=True) - 2.0 * hrow * hrow
    quad = quad + jnp.where(lane1 == at_h + count, total, 0.0)
    squared = jnp.maximum(jnp.sum(quad, 1, keepdims=True), 0.0)
    beta = jnp.sqrt(squared + 1e-06)
    inverse = 1.0 / beta
    hess[...] = jnp.where(lane1 == count, beta, hrow)[:, 0 : count + 1]
    for h in range(halves):
        fit = jnp.zeros((leaves, LANES), F32)
        for j in range(count):
            vec = bas[pl.ds(j + count * h, leaves, stride=count * halves), :]
            fit = fit + hcol[j : j + 1, :] * vec
        part = w[:, h * LANES : (h + 1) * LANES]
        out[pl.ds(h, leaves, stride=halves), :] = (part - fit) * inverse
    rest.wait_send()


def make_body(n_grp, n_leaf):
    def body(
        basis,
        roots,
        near_blocks,
        near_ids,
        leaf_basis,
        far_coupling,
        far_ids,
        transfer,
        top_coupling,
        top_ids,
    ):
        leaves, rank, width = leaf_basis.shape
        prank = transfer.shape[2]
        count = basis.shape[0]
        steps = roots.shape[0]
        n_near, n_far, n_top = near_ids.shape[1], far_ids.shape[1], top_ids.shape[1]
        n_dev = n_grp * n_leaf
        coefs = leaves * rank
        far_tiles = n_far * rank // LANES
        chunks = leaves * width // LANES
        vmem = pl.BlockSpec(memory_space=pltpu.VMEM)
        hbm = pl.BlockSpec(memory_space=pl.ANY)
        lb = leaf_basis.reshape(coefs, width)
        tr = transfer.reshape(coefs, prank)
        out, hess = pl.pallas_call(
            functools.partial(kernel, n_grp, n_leaf),
            out_shape=(
                jax.ShapeDtypeStruct((chunks, LANES), F32),
                jax.ShapeDtypeStruct((1, count + 1), F32),
            ),
            in_specs=[hbm] * 10,
            out_specs=(vmem, vmem),
            scratch_shapes=[
                pltpu.VMEM((chunks * count, LANES), F32),
                pltpu.VMEM((1, steps), F32),
                pltpu.VMEM(near_blocks.shape, BF16),
                pltpu.VMEM((leaves, n_near - 1, width, width), BF16),
                pltpu.VMEM(near_ids.shape, jnp.int32),
                pltpu.VMEM(lb.shape, BF16),
                pltpu.VMEM((width, coefs), BF16),
                pltpu.VMEM(far_coupling.shape, BF16),
                pltpu.VMEM((coefs, n_far * rank), BF16),
                pltpu.VMEM(far_ids.shape, jnp.int32),
                pltpu.VMEM(tr.shape, BF16),
                pltpu.VMEM(top_coupling.shape, BF16),
                pltpu.VMEM(top_ids.shape, jnp.int32),
                pltpu.VMEM((n_far * rank + n_top * prank, coefs), BF16),
                pltpu.VMEM((3, n_near - 1, leaves, LANES), jnp.int32),
                pltpu.VMEM((3, far_tiles, leaves, LANES), jnp.int32),
                pltpu.VMEM((3, n_top, leaves, LANES), jnp.int32),
                pltpu.VMEM((steps, leaves, width), F32),
                pltpu.VMEM((steps, 2 * leaves, LANES), F32),
                pltpu.VMEM((steps, 2, leaves, width), F32),
                pltpu.VMEM((steps, 2, 2 * leaves, LANES), F32),
                pltpu.VMEM((leaves, width), F32),
                pltpu.VMEM((leaves, width), F32),
                pltpu.VMEM((leaves, width), F32),
                pltpu.VMEM((1, LANES), F32),
                pltpu.VMEM((n_dev, 1, LANES), F32),
                pltpu.SemaphoreType.DMA((9,)),
                pltpu.SemaphoreType.DMA((leaves,)),
                pltpu.SemaphoreType.DMA((steps, 2, 2)),
                pltpu.SemaphoreType.DMA((steps, 2, 2)),
                pltpu.SemaphoreType.DMA((2,)),
                pltpu.SemaphoreType.REGULAR((max(steps, (n_dev - 1).bit_length()),)),
            ],
            compiler_params=pltpu.CompilerParams(
                collective_id=0, has_side_effects=True, vmem_limit_bytes=48 * 1024 * 1024
            ),
        )(
            *(
                pltpu.with_memory_space_constraint(operand, pltpu.HBM)
                for operand in (
                    basis,
                    roots.reshape(1, steps),
                    near_blocks,
                    near_ids,
                    lb,
                    far_coupling,
                    far_ids,
                    tr,
                    top_coupling,
                    top_ids,
                )
            )
        )
        return out.reshape(leaves * width), hess.reshape(count + 1)

    return body


def solution(mesh):
    both = ("grp", "leaf")
    return jax.shard_map(
        make_body(mesh.shape["grp"], mesh.shape["leaf"]),
        mesh=mesh,
        in_specs=(
            P(None, both),
            P(),
            P(both, None, None, None),
            P(both, None),
            P(both, None, None),
            P(both, None, None, None),
            P(both, None),
            P(both, None, None),
            P(both, None, None, None),
            P(both, None),
        ),
        out_specs=(P(both), P()),
        check_vma=False,
    )
```

```python
import functools

import jax
import jax.numpy as jnp
from jax import lax
from jax.experimental import pallas as pl
from jax.experimental.pallas import tpu as pltpu
from jax.sharding import PartitionSpec as P

MESH = pl.DeviceIdType.MESH
F32 = jnp.float32
BF16 = jnp.bfloat16
LANES = 128


def nt(a, b):
    return lax.dot_general(a, b, (((1,), (1,)), ((), ())), preferred_element_type=F32)


def nn(a, b):
    return lax.dot_general(a, b, (((1,), (0,)), ((), ())), preferred_element_type=F32)


def iota(shape, dim):
    return lax.broadcasted_iota(jnp.int32, shape, dim)


def kernel(
    n_grp,
    n_leaf,
    basis_hbm,
    roots_hbm,
    near_hbm,
    near_ids_hbm,
    lb_hbm,
    fc_hbm,
    far_ids_hbm,
    tr_hbm,
    tc_hbm,
    top_ids_hbm,
    out,
    hess,
    bas,
    roots,
    near,
    near_t,
    near_f,
    near_ids,
    lb,
    up_w,
    fc,
    fcc,
    far_ids,
    tr,
    tc,
    top_ids,
    g_w,
    top_w,
    tr_t,
    near_ix,
    far_ix,
    top_ix,
    own_x,
    own_ct,
    halo_x,
    halo_ct,
    prod_buf,
    z_buf,
    w_buf,
    gram_row,
    slots,
    load_sem,
    near_sem,
    send_sem,
    recv_sem,
    red_sem,
    ready_sem,
):
    n_dev = n_grp * n_leaf
    rounds = ready_sem.shape[0]
    n_mxu = near_t.shape[0]
    leaves, n_near, width, _ = near.shape
    n_far, rank = fc.shape[1], fc.shape[2]
    n_top, prank = tc.shape[1], tc.shape[2]
    parents = tc.shape[0]
    count = basis_hbm.shape[0]
    steps = roots.shape[1]
    mid = (n_mxu + leaves) // 2
    coefs = leaves * rank
    halves = width // LANES
    chunks = leaves * halves
    far_tiles = n_far * rank // LANES
    mg, ml = lax.axis_index("grp"), lax.axis_index("leaf")
    me = mg * n_leaf + ml

    def place(index):
        return (lax.div(index, n_leaf), lax.rem(index, n_leaf))

    odd = lax.rem(me, 2)
    fast = me + 1 - 2 * odd
    slow = me - 1 + 2 * odd
    has_slow = jnp.logical_and(slow >= 0, slow < n_dev)

    barrier = pltpu.get_barrier_semaphore()

    def around(distance, call):
        for other in (me - distance, me + distance):

            @pl.when(jnp.logical_and(other >= 0, other < n_dev))
            def _():
                call(other)

    def signal(sem, distance):
        def one(other):
            pl.semaphore_signal(sem, inc=1, device_id=place(other), device_id_type=MESH)

        around(distance, one)

    def await_signals(sem, distance):
        peers = jnp.where(me >= distance, 1, 0) + jnp.where(me + distance < n_dev, 1, 0)
        pl.semaphore_wait(sem, peers)

    signal(barrier, 1)

    first = [
        pltpu.make_async_copy(
            basis_hbm.at[:, c * LANES : (c + 1) * LANES],
            bas.at[c * count : (c + 1) * count, :],
            load_sem.at[0],
        )
        for c in range(chunks)
    ]
    all_basis = pltpu.make_async_copy(bas, bas, load_sem.at[0])
    loads = [
        pltpu.make_async_copy(src, dst, load_sem.at[1 + n])
        for n, (src, dst) in enumerate(
            (
                (roots_hbm, roots),
                (near_ids_hbm, near_ids),
                (far_ids_hbm, far_ids),
                (top_ids_hbm, top_ids),
                (lb_hbm, lb),
                (tr_hbm, tr),
                (fc_hbm, fc),
                (tc_hbm, tc),
            )
        )
    ]
    lb_copy, tr_copy, fc_copy, tc_copy = loads[4:]
    for copy in first + loads:
        copy.start()
    for i in range(leaves):
        pltpu.make_async_copy(near_hbm.at[i], near.at[i], near_sem.at[i]).start()


    row = iota((leaves, LANES), 0)
    lane = iota((leaves, LANES), 1)
    low = lane < rank
    even = row % 2 == 0
    own_base = me * leaves
    shift = (1 - 2 * odd) * leaves

    def side_tile(source, j, lo):
        return jnp.broadcast_to(source[j : j + 1, lo : lo + LANES], (leaves, LANES))

    @pl.when(jnp.logical_not(has_slow))
    def _():
        for step in range(steps):
            halo_x[step, 1] = jnp.zeros((leaves, width), F32)
            halo_ct[step, 1] = jnp.zeros((2 * leaves, LANES), F32)

    for copy in loads[:4]:
        copy.wait()
    nid = near_ids[...] - own_base
    for k in range(1, n_near):
        tile = jnp.broadcast_to(nid[:, k : k + 1], (leaves, LANES))
        near_ix[0, k - 1] = tile
        near_ix[1, k - 1] = tile - shift
        near_ix[2, k - 1] = tile + shift
    fid = far_ids[...] - own_base
    for v in range(far_tiles):
        tile = jnp.where(low, fid[:, 2 * v : 2 * v + 1], fid[:, 2 * v + 1 : 2 * v + 2])
        far_ix[0, v] = tile
        far_ix[1, v] = tile - shift
        far_ix[2, v] = tile + shift
    tid = jnp.zeros((leaves, n_top), jnp.int32)
    for p in range(parents):
        tid = jnp.where(iota((leaves, n_top), 0) // 2 == p, top_ids[p : p + 1, :], tid)
    tid = (tid - me * parents) * 2
    for k in range(n_top):
        tile = jnp.broadcast_to(tid[:, k : k + 1], (leaves, LANES))
        top_ix[0, k] = tile
        top_ix[1, k] = tile - shift
        top_ix[2, k] = tile + shift

    all_basis.wait()
    for h in range(halves):
        prod_buf[:, h * LANES : (h + 1) * LANES] = bas[
            pl.ds(count - 1 + count * h, leaves, stride=count * halves), :
        ]
    z_buf[...] = jnp.zeros_like(z_buf)

    lb_copy.wait()
    up_w[...] = lb[...].T
    tr_copy.wait()

    await_signals(barrier, 1)

    def x_copy(step, side):
        return pltpu.make_async_remote_copy(
            src_ref=own_x.at[step],
            dst_ref=halo_x.at[step, side],
            send_sem=send_sem.at[step, 0, side],
            recv_sem=recv_sem.at[step, 0, side],
            device_id=place((fast, slow)[side]),
            device_id_type=MESH,
        )

    def ct_copy(step, side):
        return pltpu.make_async_remote_copy(
            src_ref=own_ct.at[step],
            dst_ref=halo_ct.at[step, side],
            send_sem=send_sem.at[step, 1, side],
            recv_sem=recv_sem.at[step, 1, side],
            device_id=place((fast, slow)[side]),
            device_id_type=MESH,
        )

    def send(step, make):
        @pl.when(has_slow)
        def _():
            make(step, 1).start()

        make(step, 0).start()

    def receive(step, make, side):
        if side == 0:
            make(step, 0).wait_recv()
        else:

            @pl.when(has_slow)
            def _():
                make(step, 1).wait_recv()

    def pick_x(ix, source, acc):
        out = [list(a) for a in acc]
        rows = [[side_tile(source, j, h * LANES) for h in range(halves)] for j in range(leaves)]
        for k in range(n_near - 1):
            index = near_ix[ix, k]
            for j in range(leaves):
                hit = index == j
                for h in range(halves):
                    out[k][h] = jnp.where(hit, rows[j][h], out[k][h])
        return out

    def pick_ct(ix, source, far, top):
        far, top = list(far), list(top)
        for j in range(leaves):
            tile = side_tile(source, j, 0)
            for v in range(far_tiles):
                far[v] = jnp.where(far_ix[ix, v] == j, tile, far[v])
        for j in range(0, leaves, 2):
            tile = side_tile(source, leaves + j, 0)
            for k in range(n_top):
                top[k] = jnp.where(top_ix[ix, k] == j, tile, top[k])
        return far, top

    def prepare():
        fc_copy.wait()
        tc_copy.wait()

        def fold(k):
            start = pl.multiple_of(k * prank, prank)
            for p in range(parents):
                top_w[pl.ds(start, prank), p * prank : (p + 1) * prank] = tc[p, k].T

        def build(i):
            start = pl.multiple_of(i * rank, rank)
            for k in range(n_far):
                fcc[pl.ds(start, rank), k * rank : (k + 1) * rank] = fc[i, k]
            if n_top == leaves:
                fold(i)

        def turn(i, carry):
            pltpu.make_async_copy(near_hbm.at[i], near.at[i], near_sem.at[i]).wait()
            build(i)
            for k in range(1, n_near):
                near_t[i, k - 1] = near[i, k].T
            return carry

        def widen(i, carry):
            pltpu.make_async_copy(near_hbm.at[i], near.at[i], near_sem.at[i]).wait()
            build(i)
            for k in range(1, n_near):
                near_f[i - n_mxu, k - 1] = near[i, k].astype(F32)
            return carry

        lax.fori_loop(0, n_mxu, turn, 0)
        lax.fori_loop(n_mxu, leaves, widen, 0)
        if n_top != leaves:
            for k in range(n_top):
                fold(k)
        g_w[...] = fcc[...].T
        tr_t[...] = tr[...].T

    def make_gram():
        flat = jnp.concatenate(
            [bas[c * count : (c + 1) * count, :] for c in range(chunks)], 1
        )
        gram = lax.dot_general(
            flat,
            flat,
            (((1,), (1,)), ((), ())),
            precision=lax.Precision.HIGHEST,
            preferred_element_type=F32,
        )
        flip = iota((count, count), 0) + iota((count, count), 1) == count - 1
        gram = lax.dot_general(
            flip.astype(F32),
            gram,
            (((1,), (0,)), ((), ())),
            precision=lax.Precision.HIGHEST,
            preferred_element_type=F32,
        )
        gram = jnp.pad(gram, ((0, 0), (0, LANES - count)))
        spread = pltpu.roll(gram, 0, 1, stride=count, stride_axis=0)
        gram_row[...] = jnp.sum(spread, 0, keepdims=True)

    diag = iota((leaves, coefs), 0) == iota((leaves, coefs), 1) // rank
    row_w = iota((leaves, width), 0)

    def greet(step, distance):
        @pl.when(step >= 2)
        def _():
            await_signals(ready_sem.at[step - 1], distance // 2)

        signal(ready_sem.at[step], distance)
        pl.when(step == 1)(make_gram)

    def apply(step, field, early, distance):
        own_x[step] = field
        send(step, x_copy)
        xb = field.astype(BF16)
        masked = jnp.where(diag, nn(xb, up_w[...]), 0.0)
        part = masked[:, 0:LANES]
        for v in range(1, coefs // LANES):
            part = part + masked[:, v * LANES : (v + 1) * LANES]
        dup = part + pltpu.roll(part, rank, 1)
        rise = nn(masked.astype(BF16), tr[...])
        rise = rise + jnp.where(
            even, pltpu.roll(rise, leaves - 1, 0), pltpu.roll(rise, 1, 0)
        )
        own_ct[step, 0:leaves, :] = dup
        own_ct[step, leaves : 2 * leaves, :] = rise
        send(step, ct_copy)
        if early is not None:
            early()
        else:
            greet(step, distance)
        acc = 0.5 * field
        for i in range(leaves):
            acc = acc + jnp.where(row_w == i, nt(xb, near[i, 0]), 0.0)
        zero = jnp.zeros((leaves, LANES), F32)
        xs = pick_x(0, own_x.at[step], [[zero] * halves] * (n_near - 1))
        far, top = pick_ct(0, own_ct.at[step], [zero] * far_tiles, [zero] * n_top)
        receive(step, x_copy, 0)
        xs = pick_x(1, halo_x.at[step, 0], xs)
        receive(step, ct_copy, 0)
        far, top = pick_ct(1, halo_ct.at[step, 0], far, top)
        receive(step, x_copy, 1)
        xs = pick_x(2, halo_x.at[step, 1], xs)
        xs = [jnp.concatenate(x, 1).astype(BF16) for x in xs]
        rows = [x.astype(F32) for x in xs]

        def vector_tiles(i):
            return [
                [jnp.broadcast_to(x[i : i + 1, h * LANES : (h + 1) * LANES], (leaves, LANES))
                    for h in range(halves)]
                for x in rows
            ]

        def vector_group(i, tiles, top):
            r = None
            for k in range(n_near - 1):
                for h in range(halves):
                    w = near_f[i - n_mxu, k, top : top + leaves, h * LANES : (h + 1) * LANES]
                    r = w * tiles[k][h] if r is None else r + w * tiles[k][h]
            return jnp.sum(r, 1, keepdims=True)

        def near_part(acc, m_lo, m_hi, v_lo, v_hi):
            groups = [(i, top) for i in range(v_lo, v_hi) for top in range(0, width, leaves)]
            order = []
            for i in range(m_lo, m_hi, 2):
                pair = range(i, min(i + 2, m_hi))
                order += [(m, k) for k in range(n_near - 1) for m in pair]
            tiles = {i: vector_tiles(i) for i in range(v_lo, v_hi)}
            parts = {}
            sums = {}
            done = 0
            for n, (m, k) in enumerate(order):
                dot = nn(xs[k], near_t[m, k])
                sums[m] = sums[m] + dot if m in sums else dot
                upto = len(groups) * (n + 1) // len(order)
                for i, top in groups[done:upto]:
                    o = top // LANES
                    part = parts.get((i, o), jnp.zeros((leaves, LANES), F32))
                    r = vector_group(i, tiles[i], top)
                    parts[i, o] = jnp.where(lane == row + top % LANES, r, part)
                done = upto
            for m in sums:
                acc = acc + jnp.where(row_w == m, sums[m], 0.0)
            for i in range(v_lo, v_hi):
                r = [jnp.sum(parts[i, o], 0, keepdims=True) for o in range(halves)]
                acc = acc + jnp.where(row_w == i, jnp.concatenate(r, 1), 0.0)
            return acc

        acc = near_part(acc, 0, n_mxu // 2, n_mxu, mid)
        receive(step, ct_copy, 1)
        far, top = pick_ct(2, halo_ct.at[step, 1], far, top)
        tops = nn(jnp.concatenate(top, 1).astype(BF16), top_w[...])
        srow = tops[:, 0:prank]
        for p in range(1, parents):
            srow = jnp.where(row // 2 == p, tops[:, p * prank : (p + 1) * prank], srow)
        leaf_sum = nn(jnp.concatenate(far, 1).astype(BF16), g_w[...])
        down = nn(srow.astype(BF16), tr_t[...])
        g = jnp.where(diag, leaf_sum + down, 0.0).astype(BF16)
        acc = near_part(acc, n_mxu // 2, n_mxu, mid, leaves)
        return acc + nn(g, lb[...])

    def body(step, early, distance):
        root = roots[0:1, 0:1]
        for s in range(1, steps):
            root = jnp.where(step == s, roots[0:1, s : s + 1], root)
        inverse = 1.0 / root
        prod = prod_buf[...]
        z = z_buf[...] + prod * inverse
        z_buf[...] = z
        last = step == steps - 1
        field = jnp.where(last, z, prod)
        image = apply(step, field, early, distance)
        prod_buf[...] = jnp.where(last, image, prod - image * inverse)

    body(0, prepare, 1)

    def loop(step, distance):
        body(step, None, distance)
        return distance * 2

    lax.fori_loop(1, steps, loop, 2)
    await_signals(ready_sem.at[steps - 1], 2 ** (steps - 1))
    for r in range(steps, rounds):
        signal(ready_sem.at[r], 2**r)
        await_signals(ready_sem.at[r], 2**r)

    w = prod_buf[...]
    w_buf[...] = w
    proj = jnp.zeros((count, LANES), F32)
    for c in range(chunks):
        i, h = c // halves, c % halves
        proj = proj + bas[c * count : (c + 1) * count, :] * side_tile(w_buf, i, h * LANES)
    hcol = jnp.sum(proj, 1, keepdims=True)
    ww = jnp.sum(jnp.sum(w * w, 1, keepdims=True), 0, keepdims=True)
    at_h = count * count
    lane_c = iota((count, LANES), 1)
    row_c = iota((count, LANES), 0)
    lane1 = iota((1, LANES), 1)
    hsum = jnp.sum(jnp.where(lane_c == row_c + at_h, hcol, 0.0), 0, keepdims=True)
    slots[me] = gram_row[...] + hsum + jnp.where(lane1 == at_h + count, ww, 0.0)

    for g in range(n_grp):
        for l in range(n_leaf):

            @pl.when(me != g * n_leaf + l)
            def _():
                pltpu.make_async_remote_copy(
                    src_ref=slots.at[me],
                    dst_ref=slots.at[me],
                    send_sem=red_sem.at[0],
                    recv_sem=red_sem.at[1],
                    device_id=(g, l),
                    device_id_type=MESH,
                ).start()

    rest = pltpu.make_async_remote_copy(
        src_ref=slots.at[pl.ds(0, n_dev - 1)],
        dst_ref=slots.at[pl.ds(0, n_dev - 1)],
        send_sem=red_sem.at[0],
        recv_sem=red_sem.at[1],
        device_id=place(fast),
        device_id_type=MESH,
    )
    def drain(step, carry):
        for make in (x_copy, ct_copy):
            make(step, 0).wait_send()

            @pl.when(has_slow)
            def _():
                make(step, 1).wait_send()

        return carry

    lax.fori_loop(0, steps, drain, 0)
    rest.wait_recv()
    total = jnp.sum(slots[...], 0) * (1.0 / (leaves * width * n_dev))
    hrow = jnp.where(lane1 < count, pltpu.roll(total, LANES - at_h, 1), 0.0)
    hcol = jnp.sum(jnp.where(lane_c == row_c, hrow, 0.0), 1, keepdims=True)
    gram = pltpu.roll(
        jnp.broadcast_to(total, (count, LANES)),
        LANES - count * (count - 1),
        1,
        stride=count,
        stride_axis=0,
    )
    quad = jnp.sum(hcol * (gram * hrow), 0, keepdims=True) - 2.0 * hrow * hrow
    quad = quad + jnp.where(lane1 == at_h + count, total, 0.0)
    squared = jnp.maximum(jnp.sum(quad, 1, keepdims=True), 0.0)
    beta = jnp.sqrt(squared + 1e-06)
    inverse = 1.0 / beta
    hess[...] = jnp.where(lane1 == count, beta, hrow)[:, 0 : count + 1]
    for h in range(halves):
        fit = jnp.zeros((leaves, LANES), F32)
        for j in range(count):
            vec = bas[pl.ds(j + count * h, leaves, stride=count * halves), :]
            fit = fit + hcol[j : j + 1, :] * vec
        part = w[:, h * LANES : (h + 1) * LANES]
        out[pl.ds(h, leaves, stride=halves), :] = (part - fit) * inverse
    rest.wait_send()


def make_body(n_grp, n_leaf):
    def body(
        basis,
        roots,
        near_blocks,
        near_ids,
        leaf_basis,
        far_coupling,
        far_ids,
        transfer,
        top_coupling,
        top_ids,
    ):
        leaves, rank, width = leaf_basis.shape
        prank = transfer.shape[2]
        count = basis.shape[0]
        steps = roots.shape[0]
        n_near, n_far, n_top = near_ids.shape[1], far_ids.shape[1], top_ids.shape[1]
        n_dev = n_grp * n_leaf
        n_vec = leaves // 2
        coefs = leaves * rank
        far_tiles = n_far * rank // LANES
        chunks = leaves * width // LANES
        vmem = pl.BlockSpec(memory_space=pltpu.VMEM)
        hbm = pl.BlockSpec(memory_space=pl.ANY)
        lb = leaf_basis.reshape(coefs, width)
        tr = transfer.reshape(coefs, prank)
        out, hess = pl.pallas_call(
            functools.partial(kernel, n_grp, n_leaf),
            out_shape=(
                jax.ShapeDtypeStruct((chunks, LANES), F32),
                jax.ShapeDtypeStruct((1, count + 1), F32),
            ),
            in_specs=[hbm] * 10,
            out_specs=(vmem, vmem),
            scratch_shapes=[
                pltpu.VMEM((chunks * count, LANES), F32),
                pltpu.VMEM((1, steps), F32),
                pltpu.VMEM(near_blocks.shape, BF16),
                pltpu.VMEM((leaves - n_vec, n_near - 1, width, width), BF16),
                pltpu.VMEM((n_vec, n_near - 1, width, width), F32),
                pltpu.VMEM(near_ids.shape, jnp.int32),
                pltpu.VMEM(lb.shape, BF16),
                pltpu.VMEM((width, coefs), BF16),
                pltpu.VMEM(far_coupling.shape, BF16),
                pltpu.VMEM((coefs, n_far * rank), BF16),
                pltpu.VMEM(far_ids.shape, jnp.int32),
                pltpu.VMEM(tr.shape, BF16),
                pltpu.VMEM(top_coupling.shape, BF16),
                pltpu.VMEM(top_ids.shape, jnp.int32),
                pltpu.VMEM((n_far * rank, coefs), BF16),
                pltpu.VMEM((n_top * prank, leaves // 2 * prank), BF16),
                pltpu.VMEM((prank, coefs), BF16),
                pltpu.VMEM((3, n_near - 1, leaves, LANES), jnp.int32),
                pltpu.VMEM((3, far_tiles, leaves, LANES), jnp.int32),
                pltpu.VMEM((3, n_top, leaves, LANES), jnp.int32),
                pltpu.VMEM((steps, leaves, width), F32),
                pltpu.VMEM((steps, 2 * leaves, LANES), F32),
                pltpu.VMEM((steps, 2, leaves, width), F32),
                pltpu.VMEM((steps, 2, 2 * leaves, LANES), F32),
                pltpu.VMEM((leaves, width), F32),
                pltpu.VMEM((leaves, width), F32),
                pltpu.VMEM((leaves, width), F32),
                pltpu.VMEM((1, LANES), F32),
                pltpu.VMEM((n_dev, 1, LANES), F32),
                pltpu.SemaphoreType.DMA((9,)),
                pltpu.SemaphoreType.DMA((leaves,)),
                pltpu.SemaphoreType.DMA((steps, 2, 2)),
                pltpu.SemaphoreType.DMA((steps, 2, 2)),
                pltpu.SemaphoreType.DMA((2,)),
                pltpu.SemaphoreType.REGULAR((max(steps, (n_dev - 1).bit_length()),)),
            ],
            compiler_params=pltpu.CompilerParams(
                collective_id=0, has_side_effects=True, vmem_limit_bytes=48 * 1024 * 1024
            ),
        )(
            *(
                pltpu.with_memory_space_constraint(operand, pltpu.HBM)
                for operand in (
                    basis,
                    roots.reshape(1, steps),
                    near_blocks,
                    near_ids,
                    lb,
                    far_coupling,
                    far_ids,
                    tr,
                    top_coupling,
                    top_ids,
                )
            )
        )
        return out.reshape(leaves * width), hess.reshape(count + 1)

    return body


def solution(mesh):
    both = ("grp", "leaf")
    return jax.shard_map(
        make_body(mesh.shape["grp"], mesh.shape["leaf"]),
        mesh=mesh,
        in_specs=(
            P(None, both),
            P(),
            P(both, None, None, None),
            P(both, None),
            P(both, None, None),
            P(both, None, None, None),
            P(both, None),
            P(both, None, None),
            P(both, None, None, None),
            P(both, None),
        ),
        out_specs=(P(both), P()),
        check_vma=False,
    )
```

```python
import functools

import jax
import jax.numpy as jnp
from jax import lax
from jax.experimental import pallas as pl
from jax.experimental.pallas import tpu as pltpu
from jax.sharding import PartitionSpec as P

MESH = pl.DeviceIdType.MESH
F32 = jnp.float32
BF16 = jnp.bfloat16
LANES = 128


def nt(a, b):
    return lax.dot_general(a, b, (((1,), (1,)), ((), ())), preferred_element_type=F32)


def nn(a, b):
    return lax.dot_general(a, b, (((1,), (0,)), ((), ())), preferred_element_type=F32)


def iota(shape, dim):
    return lax.broadcasted_iota(jnp.int32, shape, dim)


def kernel(
    n_grp,
    n_leaf,
    basis_hbm,
    roots_hbm,
    near_hbm,
    near_ids_hbm,
    lb_hbm,
    fc_hbm,
    far_ids_hbm,
    tr_hbm,
    tc_hbm,
    top_ids_hbm,
    out,
    hess,
    bas,
    roots,
    near,
    near_t,
    near_f,
    near_ids,
    lb,
    up_w,
    fc,
    fcc,
    far_ids,
    tr,
    tc,
    top_ids,
    g_w,
    top_w,
    tr_t,
    near_ix,
    far_ix,
    top_ix,
    own_x,
    own_ct,
    halo_x,
    halo_ct,
    prod_buf,
    w_buf,
    gram_row,
    slots,
    load_sem,
    near_sem,
    send_sem,
    recv_sem,
    red_sem,
    ready_sem,
):
    n_dev = n_grp * n_leaf
    rounds = ready_sem.shape[0]
    n_mxu = near_t.shape[0]
    leaves, n_near, width, _ = near.shape
    n_far, rank = fc.shape[1], fc.shape[2]
    n_top, prank = tc.shape[1], tc.shape[2]
    parents = tc.shape[0]
    count = basis_hbm.shape[0]
    steps = roots.shape[1]
    mid = (n_mxu + leaves) // 2
    coefs = leaves * rank
    halves = width // LANES
    chunks = leaves * halves
    far_tiles = n_far * rank // LANES
    mg, ml = lax.axis_index("grp"), lax.axis_index("leaf")
    me = mg * n_leaf + ml

    def place(index):
        return (lax.div(index, n_leaf), lax.rem(index, n_leaf))

    odd = lax.rem(me, 2)
    fast = me + 1 - 2 * odd
    slow = me - 1 + 2 * odd
    has_slow = jnp.logical_and(slow >= 0, slow < n_dev)

    barrier = pltpu.get_barrier_semaphore()

    def around(distance, call):
        for other in (me - distance, me + distance):

            @pl.when(jnp.logical_and(other >= 0, other < n_dev))
            def _():
                call(other)

    def signal(sem, distance):
        def one(other):
            pl.semaphore_signal(sem, inc=1, device_id=place(other), device_id_type=MESH)

        around(distance, one)

    def await_signals(sem, distance):
        peers = jnp.where(me >= distance, 1, 0) + jnp.where(me + distance < n_dev, 1, 0)
        pl.semaphore_wait(sem, peers)

    signal(barrier, 1)

    first = [
        pltpu.make_async_copy(
            basis_hbm.at[:, c * LANES : (c + 1) * LANES],
            bas.at[c * count : (c + 1) * count, :],
            load_sem.at[0],
        )
        for c in range(chunks)
    ]
    all_basis = pltpu.make_async_copy(bas, bas, load_sem.at[0])
    loads = [
        pltpu.make_async_copy(src, dst, load_sem.at[1 + n])
        for n, (src, dst) in enumerate(
            (
                (roots_hbm, roots),
                (near_ids_hbm, near_ids),
                (far_ids_hbm, far_ids),
                (top_ids_hbm, top_ids),
                (lb_hbm, lb),
                (tr_hbm, tr),
                (fc_hbm, fc),
                (tc_hbm, tc),
            )
        )
    ]
    lb_copy, tr_copy, fc_copy, tc_copy = loads[4:]
    for copy in first + loads:
        copy.start()
    for i in range(leaves):
        pltpu.make_async_copy(near_hbm.at[i], near.at[i], near_sem.at[i]).start()


    row = iota((leaves, LANES), 0)
    lane = iota((leaves, LANES), 1)
    low = lane < rank
    even = row % 2 == 0
    own_base = me * leaves
    shift = (1 - 2 * odd) * leaves

    def side_tile(source, j, lo):
        return jnp.broadcast_to(source[j : j + 1, lo : lo + LANES], (leaves, LANES))

    @pl.when(jnp.logical_not(has_slow))
    def _():
        for step in range(steps):
            halo_x[step, 1] = jnp.zeros((leaves, width), F32)
            halo_ct[step, 1] = jnp.zeros((2 * leaves, LANES), F32)

    for copy in loads[:4]:
        copy.wait()
    nid = near_ids[...] - own_base
    for k in range(1, n_near):
        tile = jnp.broadcast_to(nid[:, k : k + 1], (leaves, LANES))
        near_ix[0, k - 1] = tile
        near_ix[1, k - 1] = tile - shift
        near_ix[2, k - 1] = tile + shift
    fid = far_ids[...] - own_base
    for v in range(far_tiles):
        tile = jnp.where(low, fid[:, 2 * v : 2 * v + 1], fid[:, 2 * v + 1 : 2 * v + 2])
        far_ix[0, v] = tile
        far_ix[1, v] = tile - shift
        far_ix[2, v] = tile + shift
    tid = jnp.zeros((leaves, n_top), jnp.int32)
    for p in range(parents):
        tid = jnp.where(iota((leaves, n_top), 0) // 2 == p, top_ids[p : p + 1, :], tid)
    tid = (tid - me * parents) * 2
    for k in range(n_top):
        tile = jnp.broadcast_to(tid[:, k : k + 1], (leaves, LANES))
        top_ix[0, k] = tile
        top_ix[1, k] = tile - shift
        top_ix[2, k] = tile + shift

    all_basis.wait()
    for h in range(halves):
        prod_buf[:, h * LANES : (h + 1) * LANES] = bas[
            pl.ds(count - 1 + count * h, leaves, stride=count * halves), :
        ]

    lb_copy.wait()
    up_w[...] = lb[...].T
    tr_copy.wait()

    await_signals(barrier, 1)

    def x_copy(step, side):
        return pltpu.make_async_remote_copy(
            src_ref=own_x.at[step],
            dst_ref=halo_x.at[step, side],
            send_sem=send_sem.at[step, 0, side],
            recv_sem=recv_sem.at[step, 0, side],
            device_id=place((fast, slow)[side]),
            device_id_type=MESH,
        )

    def ct_copy(step, side):
        return pltpu.make_async_remote_copy(
            src_ref=own_ct.at[step],
            dst_ref=halo_ct.at[step, side],
            send_sem=send_sem.at[step, 1, side],
            recv_sem=recv_sem.at[step, 1, side],
            device_id=place((fast, slow)[side]),
            device_id_type=MESH,
        )

    def send(step, make):
        @pl.when(has_slow)
        def _():
            make(step, 1).start()

        make(step, 0).start()

    def receive(step, make, side):
        if side == 0:
            make(step, 0).wait_recv()
        else:

            @pl.when(has_slow)
            def _():
                make(step, 1).wait_recv()

    def pick_x(ix, source, acc):
        out = [list(a) for a in acc]
        rows = [[side_tile(source, j, h * LANES) for h in range(halves)] for j in range(leaves)]
        for k in range(n_near - 1):
            index = near_ix[ix, k]
            for j in range(leaves):
                hit = index == j
                for h in range(halves):
                    out[k][h] = jnp.where(hit, rows[j][h], out[k][h])
        return out

    def pick_ct(ix, source, far, top):
        far, top = list(far), list(top)
        for j in range(leaves):
            tile = side_tile(source, j, 0)
            for v in range(far_tiles):
                far[v] = jnp.where(far_ix[ix, v] == j, tile, far[v])
        for j in range(0, leaves, 2):
            tile = side_tile(source, leaves + j, 0)
            for k in range(n_top):
                top[k] = jnp.where(top_ix[ix, k] == j, tile, top[k])
        return far, top

    def prepare():
        fc_copy.wait()
        tc_copy.wait()

        def fold(k):
            start = pl.multiple_of(k * prank, prank)
            for p in range(parents):
                top_w[pl.ds(start, prank), p * prank : (p + 1) * prank] = tc[p, k].T

        def build(i):
            start = pl.multiple_of(i * rank, rank)
            for k in range(n_far):
                fcc[pl.ds(start, rank), k * rank : (k + 1) * rank] = fc[i, k]
            if n_top == leaves:
                fold(i)

        def turn(i, carry):
            pltpu.make_async_copy(near_hbm.at[i], near.at[i], near_sem.at[i]).wait()
            build(i)
            for k in range(1, n_near):
                near_t[i, k - 1] = near[i, k].T
            return carry

        def widen(i, carry):
            pltpu.make_async_copy(near_hbm.at[i], near.at[i], near_sem.at[i]).wait()
            build(i)
            for k in range(1, n_near):
                near_f[i - n_mxu, k - 1] = near[i, k].astype(F32)
            return carry

        lax.fori_loop(0, n_mxu, turn, 0)
        lax.fori_loop(n_mxu, leaves, widen, 0)
        if n_top != leaves:
            for k in range(n_top):
                fold(k)
        g_w[...] = fcc[...].T
        tr_t[...] = tr[...].T

    def make_gram():
        flat = jnp.concatenate(
            [bas[c * count : (c + 1) * count, :] for c in range(chunks)], 1
        )
        gram = lax.dot_general(
            flat,
            flat,
            (((1,), (1,)), ((), ())),
            precision=lax.Precision.HIGHEST,
            preferred_element_type=F32,
        )
        flip = iota((count, count), 0) + iota((count, count), 1) == count - 1
        gram = lax.dot_general(
            flip.astype(F32),
            gram,
            (((1,), (0,)), ((), ())),
            precision=lax.Precision.HIGHEST,
            preferred_element_type=F32,
        )
        gram = jnp.pad(gram, ((0, 0), (0, LANES - count)))
        spread = pltpu.roll(gram, 0, 1, stride=count, stride_axis=0)
        gram_row[...] = jnp.sum(spread, 0, keepdims=True)

    diag = iota((leaves, coefs), 0) == iota((leaves, coefs), 1) // rank
    row_w = iota((leaves, width), 0)

    def greet(step, distance):
        if step >= 2:
            await_signals(ready_sem.at[step - 1], distance // 2)

        signal(ready_sem.at[step], distance)
        if step == 1:
            make_gram()

    def apply(step, field, early, distance):
        own_x[step] = field
        send(step, x_copy)
        xb = field.astype(BF16)
        masked = jnp.where(diag, nn(xb, up_w[...]), 0.0)
        part = masked[:, 0:LANES]
        for v in range(1, coefs // LANES):
            part = part + masked[:, v * LANES : (v + 1) * LANES]
        dup = part + pltpu.roll(part, rank, 1)
        rise = nn(masked.astype(BF16), tr[...])
        rise = rise + jnp.where(
            even, pltpu.roll(rise, leaves - 1, 0), pltpu.roll(rise, 1, 0)
        )
        own_ct[step, 0:leaves, :] = dup
        own_ct[step, leaves : 2 * leaves, :] = rise
        send(step, ct_copy)
        if early is not None:
            early()
        else:
            greet(step, distance)
        acc = 0.5 * field
        for i in range(leaves):
            acc = acc + jnp.where(row_w == i, nt(xb, near[i, 0]), 0.0)
        zero = jnp.zeros((leaves, LANES), F32)
        xs = pick_x(0, own_x.at[step], [[zero] * halves] * (n_near - 1))
        far, top = pick_ct(0, own_ct.at[step], [zero] * far_tiles, [zero] * n_top)
        receive(step, x_copy, 0)
        xs = pick_x(1, halo_x.at[step, 0], xs)
        receive(step, ct_copy, 0)
        far, top = pick_ct(1, halo_ct.at[step, 0], far, top)
        receive(step, x_copy, 1)
        xs = pick_x(2, halo_x.at[step, 1], xs)
        xs = [jnp.concatenate(x, 1).astype(BF16) for x in xs]
        rows = [x.astype(F32) for x in xs]

        def vector_tiles(i):
            return [
                [jnp.broadcast_to(x[i : i + 1, h * LANES : (h + 1) * LANES], (leaves, LANES))
                    for h in range(halves)]
                for x in rows
            ]

        def vector_group(i, tiles, top):
            r = None
            for k in range(n_near - 1):
                for h in range(halves):
                    w = near_f[i - n_mxu, k, top : top + leaves, h * LANES : (h + 1) * LANES]
                    r = w * tiles[k][h] if r is None else r + w * tiles[k][h]
            return jnp.sum(r, 1, keepdims=True)

        def near_part(acc, m_lo, m_hi, v_lo, v_hi):
            groups = [(i, top) for i in range(v_lo, v_hi) for top in range(0, width, leaves)]
            order = []
            for i in range(m_lo, m_hi, 2):
                pair = range(i, min(i + 2, m_hi))
                order += [(m, k) for k in range(n_near - 1) for m in pair]
            tiles = {i: vector_tiles(i) for i in range(v_lo, v_hi)}
            parts = {}
            sums = {}
            done = 0
            for n, (m, k) in enumerate(order):
                dot = nn(xs[k], near_t[m, k])
                sums[m] = sums[m] + dot if m in sums else dot
                upto = len(groups) * (n + 1) // len(order)
                for i, top in groups[done:upto]:
                    o = top // LANES
                    part = parts.get((i, o), jnp.zeros((leaves, LANES), F32))
                    r = vector_group(i, tiles[i], top)
                    parts[i, o] = jnp.where(lane == row + top % LANES, r, part)
                done = upto
            for m in sums:
                acc = acc + jnp.where(row_w == m, sums[m], 0.0)
            for i in range(v_lo, v_hi):
                r = [jnp.sum(parts[i, o], 0, keepdims=True) for o in range(halves)]
                acc = acc + jnp.where(row_w == i, jnp.concatenate(r, 1), 0.0)
            return acc

        acc = near_part(acc, 0, n_mxu // 2, n_mxu, mid)
        receive(step, ct_copy, 1)
        far, top = pick_ct(2, halo_ct.at[step, 1], far, top)
        tops = nn(jnp.concatenate(top, 1).astype(BF16), top_w[...])
        srow = tops[:, 0:prank]
        for p in range(1, parents):
            srow = jnp.where(row // 2 == p, tops[:, p * prank : (p + 1) * prank], srow)
        leaf_sum = nn(jnp.concatenate(far, 1).astype(BF16), g_w[...])
        down = nn(srow.astype(BF16), tr_t[...])
        g = jnp.where(diag, leaf_sum + down, 0.0).astype(BF16)
        acc = near_part(acc, n_mxu // 2, n_mxu, mid, leaves)
        return acc + nn(g, lb[...])

    inverses = [1.0 / roots[0:1, s : s + 1] for s in range(steps)]
    w = prod_buf[...]
    z = jnp.zeros_like(w)
    for step in range(steps):
        z = z + w * inverses[step]
        last = step == steps - 1
        image = apply(step, z if last else w, None if step else prepare, 2**step)
        w = image if last else w - image * inverses[step]
    await_signals(ready_sem.at[steps - 1], 2 ** (steps - 1))
    for r in range(steps, rounds):
        signal(ready_sem.at[r], 2**r)
        await_signals(ready_sem.at[r], 2**r)

    w_buf[...] = w
    proj = jnp.zeros((count, LANES), F32)
    for c in range(chunks):
        i, h = c // halves, c % halves
        proj = proj + bas[c * count : (c + 1) * count, :] * side_tile(w_buf, i, h * LANES)
    hcol = jnp.sum(proj, 1, keepdims=True)
    ww = jnp.sum(jnp.sum(w * w, 1, keepdims=True), 0, keepdims=True)
    at_h = count * count
    lane_c = iota((count, LANES), 1)
    row_c = iota((count, LANES), 0)
    lane1 = iota((1, LANES), 1)
    hsum = jnp.sum(jnp.where(lane_c == row_c + at_h, hcol, 0.0), 0, keepdims=True)
    slots[me] = gram_row[...] + hsum + jnp.where(lane1 == at_h + count, ww, 0.0)

    for g in range(n_grp):
        for l in range(n_leaf):

            @pl.when(me != g * n_leaf + l)
            def _():
                pltpu.make_async_remote_copy(
                    src_ref=slots.at[me],
                    dst_ref=slots.at[me],
                    send_sem=red_sem.at[0],
                    recv_sem=red_sem.at[1],
                    device_id=(g, l),
                    device_id_type=MESH,
                ).start()

    rest = pltpu.make_async_remote_copy(
        src_ref=slots.at[pl.ds(0, n_dev - 1)],
        dst_ref=slots.at[pl.ds(0, n_dev - 1)],
        send_sem=red_sem.at[0],
        recv_sem=red_sem.at[1],
        device_id=place(fast),
        device_id_type=MESH,
    )
    def drain(step, carry):
        for make in (x_copy, ct_copy):
            make(step, 0).wait_send()

            @pl.when(has_slow)
            def _():
                make(step, 1).wait_send()

        return carry

    lax.fori_loop(0, steps, drain, 0)
    rest.wait_recv()
    total = jnp.sum(slots[...], 0) * (1.0 / (leaves * width * n_dev))
    hrow = jnp.where(lane1 < count, pltpu.roll(total, LANES - at_h, 1), 0.0)
    hcol = jnp.sum(jnp.where(lane_c == row_c, hrow, 0.0), 1, keepdims=True)
    gram = pltpu.roll(
        jnp.broadcast_to(total, (count, LANES)),
        LANES - count * (count - 1),
        1,
        stride=count,
        stride_axis=0,
    )
    quad = jnp.sum(hcol * (gram * hrow), 0, keepdims=True) - 2.0 * hrow * hrow
    quad = quad + jnp.where(lane1 == at_h + count, total, 0.0)
    squared = jnp.maximum(jnp.sum(quad, 1, keepdims=True), 0.0)
    beta = jnp.sqrt(squared + 1e-06)
    inverse = 1.0 / beta
    hess[...] = jnp.where(lane1 == count, beta, hrow)[:, 0 : count + 1]
    for h in range(halves):
        fit = jnp.zeros((leaves, LANES), F32)
        for j in range(count):
            vec = bas[pl.ds(j + count * h, leaves, stride=count * halves), :]
            fit = fit + hcol[j : j + 1, :] * vec
        part = w[:, h * LANES : (h + 1) * LANES]
        out[pl.ds(h, leaves, stride=halves), :] = (part - fit) * inverse
    rest.wait_send()


def make_body(n_grp, n_leaf):
    def body(
        basis,
        roots,
        near_blocks,
        near_ids,
        leaf_basis,
        far_coupling,
        far_ids,
        transfer,
        top_coupling,
        top_ids,
    ):
        leaves, rank, width = leaf_basis.shape
        prank = transfer.shape[2]
        count = basis.shape[0]
        steps = roots.shape[0]
        n_near, n_far, n_top = near_ids.shape[1], far_ids.shape[1], top_ids.shape[1]
        n_dev = n_grp * n_leaf
        n_vec = leaves // 2
        coefs = leaves * rank
        far_tiles = n_far * rank // LANES
        chunks = leaves * width // LANES
        vmem = pl.BlockSpec(memory_space=pltpu.VMEM)
        hbm = pl.BlockSpec(memory_space=pl.ANY)
        lb = leaf_basis.reshape(coefs, width)
        tr = transfer.reshape(coefs, prank)
        out, hess = pl.pallas_call(
            functools.partial(kernel, n_grp, n_leaf),
            out_shape=(
                jax.ShapeDtypeStruct((chunks, LANES), F32),
                jax.ShapeDtypeStruct((1, count + 1), F32),
            ),
            in_specs=[hbm] * 10,
            out_specs=(vmem, vmem),
            scratch_shapes=[
                pltpu.VMEM((chunks * count, LANES), F32),
                pltpu.VMEM((1, steps), F32),
                pltpu.VMEM(near_blocks.shape, BF16),
                pltpu.VMEM((leaves - n_vec, n_near - 1, width, width), BF16),
                pltpu.VMEM((n_vec, n_near - 1, width, width), F32),
                pltpu.VMEM(near_ids.shape, jnp.int32),
                pltpu.VMEM(lb.shape, BF16),
                pltpu.VMEM((width, coefs), BF16),
                pltpu.VMEM(far_coupling.shape, BF16),
                pltpu.VMEM((coefs, n_far * rank), BF16),
                pltpu.VMEM(far_ids.shape, jnp.int32),
                pltpu.VMEM(tr.shape, BF16),
                pltpu.VMEM(top_coupling.shape, BF16),
                pltpu.VMEM(top_ids.shape, jnp.int32),
                pltpu.VMEM((n_far * rank, coefs), BF16),
                pltpu.VMEM((n_top * prank, leaves // 2 * prank), BF16),
                pltpu.VMEM((prank, coefs), BF16),
                pltpu.VMEM((3, n_near - 1, leaves, LANES), jnp.int32),
                pltpu.VMEM((3, far_tiles, leaves, LANES), jnp.int32),
                pltpu.VMEM((3, n_top, leaves, LANES), jnp.int32),
                pltpu.VMEM((steps, leaves, width), F32),
                pltpu.VMEM((steps, 2 * leaves, LANES), F32),
                pltpu.VMEM((steps, 2, leaves, width), F32),
                pltpu.VMEM((steps, 2, 2 * leaves, LANES), F32),
                pltpu.VMEM((leaves, width), F32),
                pltpu.VMEM((leaves, width), F32),
                pltpu.VMEM((1, LANES), F32),
                pltpu.VMEM((n_dev, 1, LANES), F32),
                pltpu.SemaphoreType.DMA((9,)),
                pltpu.SemaphoreType.DMA((leaves,)),
                pltpu.SemaphoreType.DMA((steps, 2, 2)),
                pltpu.SemaphoreType.DMA((steps, 2, 2)),
                pltpu.SemaphoreType.DMA((2,)),
                pltpu.SemaphoreType.REGULAR((max(steps, (n_dev - 1).bit_length()),)),
            ],
            compiler_params=pltpu.CompilerParams(
                collective_id=0, has_side_effects=True, vmem_limit_bytes=48 * 1024 * 1024
            ),
        )(
            *(
                pltpu.with_memory_space_constraint(operand, pltpu.HBM)
                for operand in (
                    basis,
                    roots.reshape(1, steps),
                    near_blocks,
                    near_ids,
                    lb,
                    far_coupling,
                    far_ids,
                    tr,
                    top_coupling,
                    top_ids,
                )
            )
        )
        return out.reshape(leaves * width), hess.reshape(count + 1)

    return body


def solution(mesh):
    both = ("grp", "leaf")
    return jax.shard_map(
        make_body(mesh.shape["grp"], mesh.shape["leaf"]),
        mesh=mesh,
        in_specs=(
            P(None, both),
            P(),
            P(both, None, None, None),
            P(both, None),
            P(both, None, None),
            P(both, None, None, None),
            P(both, None),
            P(both, None, None),
            P(both, None, None, None),
            P(both, None),
        ),
        out_specs=(P(both), P()),
        check_vma=False,
    )
```
